512 devices in a mesh: buyers: 32 (over y, z_lo), goods: 16 (over x, z_hi, core).
Axes of the slice: x: 4, y: 4, z: 16 (z_hi: 2, z_lo: 8; z = z_hi * 8 + z_lo), core: 2. Of those that a mesh axis runs over, the one named last changes fastest.
Arguments:
- buyer_hidden: bfloat16 [40960, 1024], P('buyers', 'goods'), may hold values from -6 to 6
- goods_hidden: bfloat16 [32768, 1024], P('goods', 'buyers'), may hold values from -6 to 6
- buyer_proj: bfloat16 [1024, 128], replicated, may hold values from -0.1875 to 0.1875
- goods_proj: bfloat16 [1024, 128], replicated, may hold values from -0.1875 to 0.1875
- endowment: float32 [40960], P('buyers'), may hold values from 0.5 to 4
Outputs:
- prices: float32 [32768], P('goods')
- utility: float32 [40960], P('buyers')
The draws below stay inside these ranges and needn't reach their ends.
All inputs are finite; a program needn't handle non-finite values.
Results may differ from the reference program's by a relative error of at most 0.0003.
The reference program's roundings to bfloat16 on the way count: a program that leaves them out, or rounds other values in their place, can miss the bound.
Values may be sent and summed in bfloat16 or wider, within the bound.
No kernel may reach another device: no remote copies, remote signals or barrier semaphores. Data moves between devices by JAX's collectives and lax.ppermute only.
A program may use at most 64 MiB of HBM per device.

```python
import math
import jax
import jax.numpy as jnp
from jax import lax

H = 1024
E = 128
BR = 1280
ITERS = 3
NB = 40960
NG = 32768
N_BUYERS = 32


def draw_buyer_hidden(key, part):
    noise_key = jax.random.fold_in(key, 11)
    block_key = jax.random.fold_in(key, 12)
    noise = jax.random.normal(noise_key, (NB, H), jnp.float32)
    directions = jax.random.normal(block_key, (NB // BR, H), jnp.float32)
    rows = 0.6 * noise + 0.8 * jnp.repeat(directions, BR, axis=0)
    return jnp.clip(rows, -6.0, 6.0).astype(jnp.bfloat16)


def draw_goods_hidden(key, part):
    noise_key = jax.random.fold_in(key, 21)
    common_key = jax.random.fold_in(key, 22)
    noise = jax.random.normal(noise_key, (NG, H), jnp.float32)
    common = jax.random.normal(common_key, (1, H), jnp.float32)
    rows = 0.8 * noise + 0.6 * common
    return jnp.clip(rows, -6.0, 6.0).astype(jnp.bfloat16)


def steps_of(key, shape, cuts, smallest, high):
    def one(position, shards_of):
        steps = jax.random.uniform(jax.random.fold_in(jax.random.fold_in(key, 6), position), (shards_of,), jnp.float32, smallest / len(cuts), high / len(cuts))
        return jnp.repeat(jnp.exp(steps), shape[position] // shards_of).reshape((-1,) + (1,) * (len(shape) - position - 1))

    level = one(*cuts[0])
    for cut in cuts[1:]:
        level = level * one(*cut)
    return level


def normal_values(own_key, dims, width, bound, kind=jnp.bfloat16):
    entries = width * jax.random.normal(own_key, dims, jnp.float32)
    return jnp.clip(entries, min=-bound, max=bound).astype(kind)


def setup_inputs(seed: int = 0) -> dict:
    key_list = jax.random.split(jax.random.key(seed), 6)
    return {
        "buyer_hidden": draw_buyer_hidden(jax.random.fold_in(key_list[5], 71), 0),
        "goods_hidden": draw_goods_hidden(jax.random.fold_in(key_list[5], 71), 0),
        "buyer_proj": normal_values(key_list[2], (H, E), H ** -0.5, 0.1875),
        "goods_proj": normal_values(key_list[3], (H, E), H ** -0.5, 0.1875),
        "endowment": jnp.clip(jnp.exp(math.log(4.0) - 2.0794415 * jax.random.uniform(key_list[4], (NB,), jnp.float32) ** steps_of(key_list[4], (NB,), ((0, 32),), -0.2, 0.2)), 0.5, 4.0),
    }


def block_values(emb_rows, goods_emb):
    scores = jnp.dot(emb_rows, goods_emb.T, preferred_element_type=jnp.float32) * (E ** -0.5)
    rounded = lax.optimization_barrier(jax.nn.softplus(scores).astype(jnp.bfloat16))
    return rounded.astype(jnp.float32)


def reference(buyer_hidden, goods_hidden, buyer_proj, goods_proj, endowment):
    buyer_emb = jnp.dot(buyer_hidden, buyer_proj, preferred_element_type=jnp.float32).astype(jnp.bfloat16)
    goods_emb = jnp.dot(goods_hidden, goods_proj, preferred_element_type=jnp.float32).astype(jnp.bfloat16)
    emb_blocks = buyer_emb.reshape(N_BUYERS, BR, E)
    spread = lax.map(lambda rows: jnp.sum(block_values(rows, goods_emb), 1), emb_blocks).reshape(NB)
    row_scale = endowment / spread
    col_scale = jnp.ones((NG,), jnp.float32)
    prices = col_scale
    utility = row_scale
    for repeat in range(ITERS):
        exponent = repeat + 1

        def price_part(inputs):
            rows, scales = inputs
            vals = block_values(rows, goods_emb)
            return jnp.sum(scales[:, None] * vals ** exponent, 0)

        prices = col_scale * jnp.sum(lax.map(price_part, (emb_blocks, row_scale.reshape(N_BUYERS, BR))), 0)
        ratio = col_scale / prices

        def utility_part(rows):
            vals = block_values(rows, goods_emb)
            return jnp.sum(vals ** (exponent + 1) * ratio[None, :], 1)

        utility = row_scale * lax.map(utility_part, emb_blocks).reshape(NB)
        if repeat + 1 < ITERS:
            row_scale = row_scale * endowment / utility
            col_scale = ratio
    return prices, utility
```

```python
import jax
import jax.numpy as jnp
from jax import lax
from jax.sharding import Mesh, PartitionSpec as P

E = 128
ITERS = 3
FINE = (("y", 4), ("zl", 8), ("x", 4), ("zh", 2), ("c", 2))
PLANE = ("y", "x", "c")
RING = ("zh", "zl")


def exchange(x, axes):
    return lax.all_to_all(x, axes, 0, 0, tiled=True)


def spread_out(x, axes, n):
    return exchange(jnp.broadcast_to(x[None], (n,) + x.shape), axes)


def per_device(buyer_hidden, goods_hidden, buyer_proj, goods_proj, endowment):
    n_plane, n_ring = 32, 16
    rows = lax.all_to_all(buyer_hidden, ("x", "zh", "c"), 0, 1, tiled=True)
    buyer_own = jnp.dot(rows, buyer_proj, preferred_element_type=jnp.float32).astype(jnp.bfloat16)
    rows = lax.all_to_all(goods_hidden, ("y", "zl"), 0, 1, tiled=True)
    goods_own = jnp.dot(rows, goods_proj, preferred_element_type=jnp.float32).astype(jnp.bfloat16)
    buyer_emb = spread_out(buyer_own, PLANE, n_plane).reshape(-1, E)
    goods_emb = spread_out(goods_own, RING, n_ring).reshape(-1, E)
    scores = lax.dot_general(
        buyer_emb, goods_emb, (((1,), (1,)), ((), ())), preferred_element_type=jnp.float32
    )
    values = jax.nn.softplus(scores * E ** (-0.5)).astype(jnp.bfloat16)
    nb, ng = values.shape

    mine = (lax.axis_index("x") * 4 + lax.axis_index("zh") * 2 + lax.axis_index("c")) * 80
    money = lax.dynamic_slice(endowment, (mine,), (80,))

    def goods_total(part):
        return jnp.sum(spread_out(part.reshape(-1, 128), PLANE, n_plane), 0).reshape(-1)

    def buyers_total(part):
        return jnp.sum(spread_out(part.reshape(-1, 128), RING, n_ring), 0).reshape(-1)

    part = jnp.sum(values, axis=1, dtype=jnp.float32)
    got = spread_out(jnp.concatenate([part, money, jnp.zeros((48,), jnp.float32)]).reshape(-1, 128), PLANE, n_plane)
    spread = jnp.sum(got[:, :20], 0).reshape(-1)
    money = got[:, 20, :80].reshape(-1)

    bid_block = (money / spread)[:, None] * values
    for repeat in range(ITERS):
        prices = buyers_total(jnp.sum(bid_block, 0))
        shares = bid_block / prices[None, :]
        part = jnp.sum(values * shares, 1)
        if repeat + 1 < ITERS:
            utility = goods_total(part)
            bid_block = (money / utility)[:, None] * values * shares
    half = lax.dynamic_slice(prices, (lax.axis_index("zh") * 512,), (512,))
    prices = spread_out(half.reshape(4, 128), ("y",), 4).reshape(-1)
    sent = jnp.broadcast_to(part.reshape(1, 4, 1, 5, 128), (2, 4, 8, 5, 128)).reshape(64, 5, 128)
    got = exchange(sent, ("zh", "y", "x", "c")).reshape(2, 32, 640)
    utility = jnp.sum(got, 1).reshape(2, 4, 160).transpose(1, 0, 2).reshape(-1)
    return (prices, utility)


def solution(mesh):
    fine = Mesh(mesh.devices.reshape([n for _, n in FINE]), [a for a, _ in FINE])
    buyers, goods = ("y", "zl"), ("x", "zh", "c")
    placed = (P(buyers, goods), P(goods, buyers), P(), P(), P(buyers))
    return jax.shard_map(
        per_device, mesh=fine, in_specs=placed, out_specs=(P(goods), P(buyers)), check_vma=False
    )
```

```python
import functools

import jax
import jax.numpy as jnp
from jax import lax
from jax.experimental import pallas as pl
from jax.experimental.pallas import tpu as pltpu
from jax.sharding import Mesh, PartitionSpec as P

ITERS = 3
FINE = (("y", 4), ("zl", 8), ("x", 4), ("zh", 2), ("c", 2))
PLANE = ("y", "x", "c")
RING = ("zh", "zl")
E = 128
NBUY = 2560
NGOOD = 1024
LB = NBUY // 128
GT = NGOOD // 128


def softplus(x):
    return jnp.maximum(x, 0.0) + jnp.log1p(jnp.exp(-jnp.abs(x)))


def values_kernel(goods_ref, buyers_ref, money_ref, values_ref, out_ref, total, rows):
    step = pl.program_id(0)

    @pl.when(step == 0)
    def _():
        total[...] = jnp.zeros_like(total)

    for b in range(NBUY // 256):
        cols = slice(256 * b, 256 * b + 256)
        scores = lax.dot_general(
            goods_ref[...], buyers_ref[cols, :], (((1,), (1,)), ((), ())), preferred_element_type=jnp.float32
        )
        rounded = softplus(scores * E ** (-0.5)).astype(jnp.bfloat16)
        values_ref[:, cols] = rounded
        total[:, cols] += jnp.sum(rounded.astype(jnp.float32).reshape(-1, 8, 256), 0)

    @pl.when(step == pl.num_programs(0) - 1)
    def _():
        whole = jnp.sum(total[...], 0, keepdims=True)
        for b in range(LB):
            rows[b : b + 1, :] = whole[:, 128 * b : 128 * b + 128]
        rows[LB : LB + 1, :] = money_ref[...]
        for p in range(out_ref.shape[0]):
            out_ref[p] = rows[0 : LB + 1, :]


def powered(v, k):
    square = v * v if k >= 2 else None
    return {1: lambda: v, 2: lambda: square, 3: lambda: square * v, 4: lambda: square * square}[k]()


def fetch(values_hbm, values, sems):
    copies = [
        pltpu.make_async_copy(values_hbm.at[pl.ds(128 * q, 128)], values.at[pl.ds(128 * q, 128)], sems.at[q])
        for q in range(GT)
    ]
    for copy in copies:
        copy.start()
    return copies


def price_kernel(k, got_ref, money_ref, values_hbm, out_ref, values, scale, sums, sems):
    copies = fetch(values_hbm, values, sems)
    total = got_ref[0, 0:LB, :]
    for p in range(1, got_ref.shape[0]):
        total = total + got_ref[p, 0:LB, :]
    scale[...] = money_ref[...] / total
    for q in range(GT):
        copies[q].wait()

        def chunk(i, _, q=q):
            at = pl.multiple_of(128 * q + 16 * i, 16)
            acc = None
            for b in range(LB):
                v = values[pl.ds(at, 16), 128 * b : 128 * b + 128].astype(jnp.float32)
                term = powered(v, k) * scale[b : b + 1, :]
                acc = term if acc is None else acc + term
            sums[pl.ds(pl.multiple_of(16 * i, 16), 16), :] = acc
            return 0

        lax.fori_loop(0, 8, chunk, 0, unroll=2)
        row = jnp.sum(sums[...].T, 0, keepdims=True)
        for p in range(out_ref.shape[0]):
            out_ref[p, q : q + 1, :] = row


def utility_kernel(k, got_ref, *refs):
    last = k == ITERS
    if last:
        before_ref, zh_ref, values_hbm, out_ref, values, inverse, spare, sems = refs
    else:
        values_hbm, out_ref, sum_ref, values, inverse, spare, sems = refs
    copies = fetch(values_hbm, values, sems)
    total = got_ref[0]
    for p in range(1, got_ref.shape[0]):
        total = total + got_ref[p]
    inverse[...] = 1.0 / total
    if last:
        spare[0:8, :] = total / before_ref[...]
        half = spare[pl.ds(pl.multiple_of(4 * zh_ref[0], 4), 4), :]
        for p in range(out_ref.shape[0]):
            out_ref[p, LB : LB + 4, :] = half
    else:
        sum_ref[...] = total
    accs = tuple(jnp.zeros((8, 128), jnp.float32) for _ in range(LB))
    for q in range(GT):
        copies[q].wait()
        spare[...] = jnp.broadcast_to(inverse[q : q + 1, :], (128, 128)).T

        def chunk(i, accs, q=q):
            at = pl.multiple_of(128 * q + 16 * i, 16)
            c = spare[pl.ds(pl.multiple_of(16 * i, 16), 16), :]
            new = []
            for b in range(LB):
                v = values[pl.ds(at, 16), 128 * b : 128 * b + 128].astype(jnp.float32)
                term = powered(v, k + 1) * c
                new.append(accs[b] + (term[0:8] + term[8:16]))
            return tuple(new)

        accs = lax.fori_loop(0, 8, chunk, accs)
    for b in range(LB):
        spare[b : b + 1, :] = jnp.sum(accs[b], 0, keepdims=True)
    for p in range(out_ref.shape[0]):
        out_ref[p, 0:LB, :] = spare[0:LB, :]


VM = pl.BlockSpec(memory_space=pltpu.VMEM)
PARAMS = pltpu.CompilerParams(vmem_limit_bytes=16 << 20)


def values_call(goods_emb, buyer_emb, money_row):
    return pl.pallas_call(
        values_kernel,
        grid=(GT,),
        in_specs=[
            pl.BlockSpec((128, E), lambda i: (i, 0)),
            pl.BlockSpec((NBUY, E), lambda i: (0, 0)),
            pl.BlockSpec((1, 128), lambda i: (0, 0)),
        ],
        out_specs=[
            pl.BlockSpec((128, NBUY), lambda i: (i, 0)),
            pl.BlockSpec((32, LB + 1, 128), lambda i: (0, 0, 0)),
        ],
        out_shape=[
            jax.ShapeDtypeStruct((NGOOD, NBUY), jnp.bfloat16),
            jax.ShapeDtypeStruct((32, LB + 1, 128), jnp.float32),
        ],
        scratch_shapes=[pltpu.VMEM((8, NBUY), jnp.float32), pltpu.VMEM((24, 128), jnp.float32)],
        compiler_params=PARAMS,
    )(goods_emb, buyer_emb, money_row)


def held():
    return pltpu.VMEM((NGOOD, NBUY), jnp.bfloat16)


def price_call(k, got, money, values):
    return pl.pallas_call(
        functools.partial(price_kernel, k),
        in_specs=[VM, VM, pl.BlockSpec(memory_space=pl.ANY)],
        out_specs=VM,
        out_shape=jax.ShapeDtypeStruct((16, GT, 128), jnp.float32),
        scratch_shapes=[
            held(),
            pltpu.VMEM((LB, 128), jnp.float32),
            pltpu.VMEM((128, 128), jnp.float32),
            pltpu.SemaphoreType.DMA((GT,)),
        ],
        compiler_params=PARAMS,
    )(got, money, values)


def utility_call(k, got, values, before=None, zh=None):
    last = k == ITERS
    scratch = [held(), pltpu.VMEM((GT, 128), jnp.float32), pltpu.VMEM((128, 128), jnp.float32), pltpu.SemaphoreType.DMA((GT,))]
    if last:
        return pl.pallas_call(
            functools.partial(utility_kernel, k),
            in_specs=[VM, VM, pl.BlockSpec(memory_space=pltpu.SMEM), pl.BlockSpec(memory_space=pl.ANY)],
            out_specs=VM,
            out_shape=jax.ShapeDtypeStruct((32, LB + 4, 128), jnp.float32),
            scratch_shapes=scratch,
            compiler_params=PARAMS,
        )(got, before, zh, values)
    return pl.pallas_call(
        functools.partial(utility_kernel, k),
        in_specs=[VM, pl.BlockSpec(memory_space=pl.ANY)],
        out_specs=[VM, VM],
        out_shape=[jax.ShapeDtypeStruct((32, LB, 128), jnp.float32), jax.ShapeDtypeStruct((GT, 128), jnp.float32)],
        scratch_shapes=scratch,
        compiler_params=PARAMS,
    )(got, values)


def exchange(x, axes):
    return lax.all_to_all(x, axes, 0, 0, tiled=True)


def spread_out(x, axes, n):
    return exchange(jnp.broadcast_to(x[None], (n,) + x.shape), axes)


def per_device(buyer_hidden, goods_hidden, buyer_proj, goods_proj, endowment):
    x, y, zh, c = (lax.axis_index(a) for a in ("x", "y", "zh", "c"))
    rows = lax.all_to_all(buyer_hidden, ("x", "zh", "c"), 0, 1, tiled=True)
    buyer_own = jnp.dot(rows, buyer_proj, preferred_element_type=jnp.float32).astype(jnp.bfloat16)
    rows = lax.all_to_all(goods_hidden, ("y", "zl"), 0, 1, tiled=True)
    goods_own = jnp.dot(rows, goods_proj, preferred_element_type=jnp.float32).astype(jnp.bfloat16)
    buyer_emb = spread_out(buyer_own, PLANE, 32).reshape(-1, E)
    goods_emb = spread_out(goods_own, RING, 16).reshape(-1, E)

    mine = lax.dynamic_index_in_dim(endowment.reshape(4, 2, 160), zh, 1, keepdims=False).reshape(5, 128)
    money_row = lax.dynamic_slice(mine, (jnp.minimum(x * 2 + c, 4), 0), (1, 128))

    values, sent = values_call(goods_emb, buyer_emb, money_row)
    got = exchange(sent, PLANE)
    money = got[:, LB].reshape(4, 8, 128)[:, :5].reshape(LB, 128)
    for k in range(1, ITERS):
        ring = exchange(price_call(k, got, money, values), RING)
        sent, before = utility_call(k, ring, values)
        got = exchange(sent, PLANE)
    ring = exchange(price_call(ITERS, got, money, values), RING)
    final = exchange(utility_call(ITERS, ring, values, before, zh.reshape(1).astype(jnp.int32)), PLANE)
    prices = lax.dynamic_index_in_dim(final.reshape(4, 8, LB + 4, 128), x * 2 + c, 1, keepdims=False)[:, LB:].reshape(-1)
    five = lambda a, axis: lax.dynamic_slice_in_dim(a, 5 * y, 5, axis)
    mine_total = jnp.sum(five(final, 1), 0) * five(money, 0) / jnp.sum(five(got, 1), 0)
    other = lax.ppermute(mine_total, "zh", [(0, 1), (1, 0)])
    first = jnp.where(zh == 0, mine_total, other).reshape(4, 160)
    second = jnp.where(zh == 0, other, mine_total).reshape(4, 160)
    utility = jnp.stack([first, second], 1).reshape(-1)
    return (prices, utility)


def solution(mesh):
    fine = Mesh(mesh.devices.reshape([n for _, n in FINE]), [a for a, _ in FINE])
    buyers, goods = ("y", "zl"), ("x", "zh", "c")
    placed = (P(buyers, goods), P(goods, buyers), P(), P(), P(buyers))
    return jax.shard_map(
        per_device, mesh=fine, in_specs=placed, out_specs=(P(goods), P(buyers)), check_vma=False
    )
```

```python
import functools

import jax
import jax.numpy as jnp
from jax import lax
from jax.experimental import pallas as pl
from jax.experimental.pallas import tpu as pltpu
from jax.sharding import Mesh, PartitionSpec as P

ITERS = 3
FINE = (("y", 4), ("zl", 8), ("x", 4), ("zh", 2), ("c", 2))
PLANE = ("y", "x", "c")
RING = ("zh", "zl")
E = 128
NBUY = 2560
NGOOD = 1024
LB = NBUY // 128
GT = NGOOD // 128


def softplus(x):
    return jnp.maximum(x, 0.0) + jnp.log1p(jnp.exp(-jnp.abs(x)))


def values_kernel(goods_ref, buyers_ref, money_ref, values_ref, out_ref, total, rows):
    step = pl.program_id(0)

    @pl.when(step == 0)
    def _():
        total[...] = jnp.zeros_like(total)

    for b in range(NBUY // 256):
        cols = slice(256 * b, 256 * b + 256)
        scores = lax.dot_general(
            goods_ref[...], buyers_ref[cols, :], (((1,), (1,)), ((), ())), preferred_element_type=jnp.float32
        )
        rounded = softplus(scores * E ** (-0.5)).astype(jnp.bfloat16)
        values_ref[:, cols] = rounded
        total[:, cols] += jnp.sum(rounded.astype(jnp.float32).reshape(-1, 8, 256), 0)

    @pl.when(step == pl.num_programs(0) - 1)
    def _():
        whole = jnp.sum(total[...], 0, keepdims=True)
        for b in range(LB):
            rows[b : b + 1, :] = whole[:, 128 * b : 128 * b + 128]
        rows[LB : LB + 1, :] = money_ref[...]
        for p in range(out_ref.shape[0]):
            out_ref[p] = rows[0 : LB + 1, :]


def powered(v, k):
    square = v * v if k >= 2 else None
    return {1: lambda: v, 2: lambda: square, 3: lambda: square * v, 4: lambda: square * square}[k]()


def price_kernel(k, got_ref, money_ref, values, out_ref, scale, sums):
    total = got_ref[0, 0:LB, :]
    for p in range(1, got_ref.shape[0]):
        total = total + got_ref[p, 0:LB, :]
    scale[...] = money_ref[...] / total
    for q in range(GT):

        def chunk(i, _, q=q):
            at = pl.multiple_of(128 * q + 16 * i, 16)
            acc = None
            for b in range(LB):
                v = values[pl.ds(at, 16), 128 * b : 128 * b + 128].astype(jnp.float32)
                term = powered(v, k) * scale[b : b + 1, :]
                acc = term if acc is None else acc + term
            sums[pl.ds(pl.multiple_of(16 * i, 16), 16), :] = acc
            return 0

        lax.fori_loop(0, 8, chunk, 0, unroll=2)
        row = jnp.sum(sums[...].T, 0, keepdims=True)
        for p in range(out_ref.shape[0]):
            out_ref[p, q : q + 1, :] = row


def utility_kernel(k, got_ref, *refs):
    last = k == ITERS
    if last:
        before_ref, zh_ref, values, out_ref, inverse, spare = refs
    else:
        values, out_ref, sum_ref, inverse, spare = refs
    total = got_ref[0]
    for p in range(1, got_ref.shape[0]):
        total = total + got_ref[p]
    inverse[...] = 1.0 / total
    if last:
        spare[0:8, :] = total / before_ref[...]
        half = spare[pl.ds(pl.multiple_of(4 * zh_ref[0], 4), 4), :]
        for p in range(out_ref.shape[0]):
            out_ref[p, LB : LB + 4, :] = half
    else:
        sum_ref[...] = total
    accs = tuple(jnp.zeros((8, 128), jnp.float32) for _ in range(LB))
    for q in range(GT):
        spare[...] = jnp.broadcast_to(inverse[q : q + 1, :], (128, 128)).T

        def chunk(i, accs, q=q):
            at = pl.multiple_of(128 * q + 16 * i, 16)
            c = spare[pl.ds(pl.multiple_of(16 * i, 16), 16), :]
            new = []
            for b in range(LB):
                v = values[pl.ds(at, 16), 128 * b : 128 * b + 128].astype(jnp.float32)
                term = powered(v, k + 1) * c
                new.append(accs[b] + (term[0:8] + term[8:16]))
            return tuple(new)

        accs = lax.fori_loop(0, 8, chunk, accs)
    for b in range(LB):
        spare[b : b + 1, :] = jnp.sum(accs[b], 0, keepdims=True)
    for p in range(out_ref.shape[0]):
        out_ref[p, 0:LB, :] = spare[0:LB, :]


VM = pl.BlockSpec(memory_space=pltpu.VMEM)
PARAMS = pltpu.CompilerParams(vmem_limit_bytes=16 << 20)


def values_call(goods_emb, buyer_emb, money_row):
    return pl.pallas_call(
        values_kernel,
        grid=(GT,),
        in_specs=[
            pl.BlockSpec((128, E), lambda i: (i, 0)),
            pl.BlockSpec((NBUY, E), lambda i: (0, 0)),
            pl.BlockSpec((1, 128), lambda i: (0, 0)),
        ],
        out_specs=[
            pl.BlockSpec((128, NBUY), lambda i: (i, 0)),
            pl.BlockSpec((32, LB + 1, 128), lambda i: (0, 0, 0)),
        ],
        out_shape=[
            jax.ShapeDtypeStruct((NGOOD, NBUY), jnp.bfloat16),
            jax.ShapeDtypeStruct((32, LB + 1, 128), jnp.float32),
        ],
        scratch_shapes=[pltpu.VMEM((8, NBUY), jnp.float32), pltpu.VMEM((24, 128), jnp.float32)],
        compiler_params=pltpu.CompilerParams(vmem_limit_bytes=61 << 20),
    )(goods_emb, buyer_emb, money_row)


def price_call(k, got, money, values):
    return pl.pallas_call(
        functools.partial(price_kernel, k),
        in_specs=[VM, VM, VM],
        out_specs=VM,
        out_shape=jax.ShapeDtypeStruct((16, GT, 128), jnp.float32),
        scratch_shapes=[
            pltpu.VMEM((LB, 128), jnp.float32),
            pltpu.VMEM((128, 128), jnp.float32),
        ],
        compiler_params=PARAMS,
    )(got, money, values)


def utility_call(k, got, values, before=None, zh=None):
    last = k == ITERS
    scratch = [pltpu.VMEM((GT, 128), jnp.float32), pltpu.VMEM((128, 128), jnp.float32)]
    if last:
        return pl.pallas_call(
            functools.partial(utility_kernel, k),
            in_specs=[VM, VM, pl.BlockSpec(memory_space=pltpu.SMEM), VM],
            out_specs=VM,
            out_shape=jax.ShapeDtypeStruct((32, LB + 4, 128), jnp.float32),
            scratch_shapes=scratch,
            compiler_params=PARAMS,
        )(got, before, zh, values)
    return pl.pallas_call(
        functools.partial(utility_kernel, k),
        in_specs=[VM, VM],
        out_specs=[VM, VM],
        out_shape=[jax.ShapeDtypeStruct((32, LB, 128), jnp.float32), jax.ShapeDtypeStruct((GT, 128), jnp.float32)],
        scratch_shapes=scratch,
        compiler_params=PARAMS,
    )(got, values)


def pack_kernel(hidden_ref, out_ref):
    rows = hidden_ref[...].T
    for q in range(8):
        at = 80 * (4 * (q // 2) + q % 2)
        out_ref[q] = jnp.concatenate([rows[at : at + 80], rows[at + 160 : at + 240]], 1)


def half_kernel(zh_ref, got_ref, proj_ref, mine_ref, other_ref, weights, both):
    weights[...] = jnp.zeros_like(weights)
    total = jnp.zeros((80, 2 * E), jnp.float32)
    for q in range(8):
        weights[q, 0:64, 0:E] = proj_ref[q]
        weights[q, 64:128, E : 2 * E] = proj_ref[q]
        total = total + jnp.dot(got_ref[q], weights[q], preferred_element_type=jnp.float32)
    both[0] = total[:, 0:E]
    both[1] = total[:, E : 2 * E]
    mine_ref[...] = both[zh_ref[0]]
    other_ref[...] = both[1 - zh_ref[0]]


def join_kernel(mine_ref, came_ref, out_ref):
    emb = (mine_ref[...] + came_ref[...]).astype(jnp.bfloat16)
    for p in range(out_ref.shape[0]):
        out_ref[p] = emb


def turn_kernel(got_ref, out_ref):
    for s in range(4):
        rows = got_ref[s].T
        for q in range(8):
            out_ref[q, :, 32 * s : 32 * s + 32] = rows[64 * q : 64 * q + 64]


def goods_kernel(got_ref, proj_ref, out_ref):
    total = jnp.dot(got_ref[0], proj_ref[0], preferred_element_type=jnp.float32)
    for q in range(1, 8):
        total = total + jnp.dot(got_ref[q], proj_ref[q], preferred_element_type=jnp.float32)
    emb = total.astype(jnp.bfloat16)
    for p in range(out_ref.shape[0]):
        out_ref[p] = emb


def small_call(kernel, outs, *args, scratch=(), smem=0):
    return pl.pallas_call(
        kernel,
        in_specs=[pl.BlockSpec(memory_space=pltpu.SMEM)] * smem + [VM] * (len(args) - smem),
        out_specs=jax.tree.map(lambda _: VM, outs),
        out_shape=outs,
        scratch_shapes=list(scratch),
        compiler_params=PARAMS,
    )(*args)


def exchange(x, axes):
    return lax.all_to_all(x, axes, 0, 0, tiled=True)


def embeddings(buyer_hidden, goods_hidden, buyer_proj, goods_proj, zh):
    bf16, f32 = jnp.bfloat16, jnp.float32
    shape = jax.ShapeDtypeStruct
    goods_part = exchange(goods_hidden.T.reshape(32, 4, 512).transpose(1, 0, 2), ("y",))
    packed = small_call(pack_kernel, shape((8, 80, 128), bf16), buyer_hidden.T)
    buyer_part = exchange(packed, ("x", "c"))
    goods_rows = exchange(small_call(turn_kernel, shape((8, 64, 128), bf16), goods_part), ("zl",))
    proj = lax.dynamic_index_in_dim(buyer_proj.reshape(4, 2, 2, 64, E), zh, 1, keepdims=False).reshape(8, 64, E)
    mine, other = small_call(
        half_kernel, (shape((80, E), f32),) * 2, zh.reshape(1), buyer_part, proj,
        scratch=(pltpu.VMEM((8, 128, 2 * E), bf16), pltpu.VMEM((2, 80, E), f32)), smem=1,
    )
    came = lax.ppermute(other, "zh", [(0, 1), (1, 0)])
    buyer_emb = exchange(small_call(join_kernel, shape((32, 80, E), bf16), mine, came), PLANE)
    proj = goods_proj.reshape(4, 8, 32, E).transpose(1, 0, 2, 3).reshape(8, 128, E)
    goods_emb = exchange(small_call(goods_kernel, shape((16, 64, E), bf16), goods_rows, proj), RING)
    return buyer_emb.reshape(-1, E), goods_emb.reshape(-1, E)


def per_device(buyer_hidden, goods_hidden, buyer_proj, goods_proj, endowment):
    x, y, zh, c = (lax.axis_index(a) for a in ("x", "y", "zh", "c"))
    buyer_emb, goods_emb = embeddings(buyer_hidden, goods_hidden, buyer_proj, goods_proj, zh)

    mine = lax.dynamic_index_in_dim(endowment.reshape(4, 2, 160), zh, 1, keepdims=False).reshape(5, 128)
    money_row = lax.dynamic_slice(mine, (jnp.minimum(x * 2 + c, 4), 0), (1, 128))

    values, sent = values_call(goods_emb, buyer_emb, money_row)
    got = exchange(sent, PLANE)
    money = got[:, LB].reshape(4, 8, 128)[:, :5].reshape(LB, 128)
    for k in range(1, ITERS):
        ring = exchange(price_call(k, got, money, values), RING)
        sent, before = utility_call(k, ring, values)
        got = exchange(sent, PLANE)
    ring = exchange(price_call(ITERS, got, money, values), RING)
    final = exchange(utility_call(ITERS, ring, values, before, zh.reshape(1)), PLANE)
    prices = lax.dynamic_index_in_dim(final.reshape(4, 8, LB + 4, 128), x * 2 + c, 1, keepdims=False)[:, LB:].reshape(-1)
    five = lambda a, axis: lax.dynamic_slice_in_dim(a, 5 * y, 5, axis)
    mine_total = jnp.sum(five(final, 1), 0) * five(money, 0) / jnp.sum(five(got, 1), 0)
    other = lax.ppermute(mine_total, "zh", [(0, 1), (1, 0)])
    first = jnp.where(zh == 0, mine_total, other).reshape(4, 160)
    second = jnp.where(zh == 0, other, mine_total).reshape(4, 160)
    utility = jnp.stack([first, second], 1).reshape(-1)
    return (prices, utility)


def solution(mesh):
    fine = Mesh(mesh.devices.reshape([n for _, n in FINE]), [a for a, _ in FINE])
    buyers, goods = ("y", "zl"), ("x", "zh", "c")
    placed = (P(buyers, goods), P(goods, buyers), P(), P(), P(buyers))
    return jax.shard_map(
        per_device, mesh=fine, in_specs=placed, out_specs=(P(goods), P(buyers)), check_vma=False
    )
```

```python
import functools

import jax
import jax.numpy as jnp
from jax import lax
from jax.experimental import pallas as pl
from jax.experimental.pallas import tpu as pltpu
from jax.sharding import Mesh, PartitionSpec as P

ITERS = 3
FINE = (("y", 4), ("zl", 8), ("x", 4), ("zh", 2), ("c", 2))
PLANE = ("y", "x", "c")
RING = ("zh", "zl")


E = 128
NBUY = 2560
NGOOD = 1024
LB = NBUY // 128
GT = NGOOD // 128


LOG2E = 1.4426950408889634
LN2 = 0.6931471805599453


def softplus_of(products):
    t = products * (E ** (-0.5) * LOG2E)
    up = jnp.maximum(t, 0.0)
    u = jnp.exp2(jnp.minimum(t, 0.0) - up)
    small = u * (LOG2E - (0.5 * LOG2E) * u)
    return (up + jnp.where(u < 2.0**-8, small, jnp.log2(1.0 + u))) * LN2


def values_kernel(goods_ref, buyers_ref, money_ref, values_ref, out_ref, total, rows):
    step = pl.program_id(0)

    @pl.when(step == 0)
    def _():
        total[...] = jnp.zeros_like(total)

    ones = jnp.ones((8, 128), jnp.bfloat16)
    for b in range(NBUY // 256):
        cols = slice(256 * b, 256 * b + 256)
        scores = lax.dot_general(
            goods_ref[...], buyers_ref[cols, :], (((1,), (1,)), ((), ())), preferred_element_type=jnp.float32
        )
        rounded = softplus_of(scores).astype(jnp.bfloat16)
        values_ref[:, cols] = rounded
        total[:, cols] += jnp.dot(ones, rounded, preferred_element_type=jnp.float32)

    @pl.when(step == pl.num_programs(0) - 1)
    def _():
        for b in range(LB):
            rows[b : b + 1, :] = total[0:1, 128 * b : 128 * b + 128]
        rows[LB : LB + 1, :] = money_ref[...]
        for p in range(out_ref.shape[0]):
            out_ref[p] = rows[0 : LB + 1, :]


def powered(v, k):
    square = v * v if k >= 2 else None
    return {1: lambda: v, 2: lambda: square, 3: lambda: square * v, 4: lambda: square * square}[k]()


def price_kernel(k, got_ref, *refs):
    if k == 1:
        values, out_ref, money_ref, scale, sums = refs
        for y in range(4):
            for i in range(5):
                money_ref[5 * y + i : 5 * y + i + 1, :] = got_ref[8 * y + i, LB : LB + 1, :]
    else:
        money_ref, values, out_ref, scale, sums = refs
    total = got_ref[0, 0:LB, :]
    for p in range(1, got_ref.shape[0]):
        total = total + got_ref[p, 0:LB, :]
    scale[...] = money_ref[...] / total
    for q in range(GT):

        def chunk(i, _, q=q):
            at = pl.multiple_of(128 * q + 16 * i, 16)
            acc = None
            for b in range(LB):
                v = values[pl.ds(at, 16), 128 * b : 128 * b + 128].astype(jnp.float32)
                term = powered(v, k) * scale[b : b + 1, :]
                acc = term if acc is None else acc + term
            sums[pl.ds(pl.multiple_of(16 * i, 16), 16), :] = acc
            return 0

        lax.fori_loop(0, 8, chunk, 0, unroll=2)
        row = jnp.sum(sums[...].T, 0, keepdims=True)
        for p in range(out_ref.shape[0]):
            out_ref[p, q : q + 1, :] = row


def utility_kernel(k, got_ref, *refs):
    last = k == ITERS
    if last:
        before_ref, zh_ref, values, out_ref, prices_ref, inverse, spare = refs
    else:
        values, out_ref, sum_ref, inverse, spare = refs
    total = got_ref[0]
    for p in range(1, got_ref.shape[0]):
        total = total + got_ref[p]
    inverse[...] = 1.0 / total
    if last:
        spare[0:8, :] = total / before_ref[...]
        half = spare[pl.ds(pl.multiple_of(4 * zh_ref[0], 4), 4), :]
        for p in range(prices_ref.shape[0]):
            prices_ref[p] = half
    else:
        sum_ref[...] = total
    accs = tuple(jnp.zeros((8, 128), jnp.float32) for _ in range(LB))
    for q in range(GT):
        spare[...] = jnp.broadcast_to(inverse[q : q + 1, :], (128, 128)).T

        def chunk(i, accs, q=q):
            at = pl.multiple_of(128 * q + 16 * i, 16)
            c = spare[pl.ds(pl.multiple_of(16 * i, 16), 16), :]
            new = []
            for b in range(LB):
                v = values[pl.ds(at, 16), 128 * b : 128 * b + 128].astype(jnp.float32)
                term = powered(v, k + 1) * c
                new.append(accs[b] + (term[0:8] + term[8:16]))
            return tuple(new)

        accs = lax.fori_loop(0, 8, chunk, accs)
    for b in range(LB):
        spare[b : b + 1, :] = jnp.sum(accs[b], 0, keepdims=True)
    for p in range(out_ref.shape[0]):
        out_ref[p] = spare[5 * (p // 8) : 5 * (p // 8) + 5, :] if last else spare[0:LB, :]


VM = pl.BlockSpec(memory_space=pltpu.VMEM)
PARAMS = pltpu.CompilerParams(vmem_limit_bytes=16 << 20)


def values_call(goods_emb, buyer_emb, money_row):
    return pl.pallas_call(
        values_kernel,
        grid=(GT,),
        in_specs=[
            pl.BlockSpec((128, E), lambda i: (i, 0)),
            pl.BlockSpec((NBUY, E), lambda i: (0, 0)),
            pl.BlockSpec((1, 128), lambda i: (0, 0)),
        ],
        out_specs=[
            pl.BlockSpec((128, NBUY), lambda i: (i, 0)),
            pl.BlockSpec((32, LB + 1, 128), lambda i: (0, 0, 0)),
        ],
        out_shape=[
            jax.ShapeDtypeStruct((NGOOD, NBUY), jnp.bfloat16),
            jax.ShapeDtypeStruct((32, LB + 1, 128), jnp.float32),
        ],
        scratch_shapes=[pltpu.VMEM((8, NBUY), jnp.float32), pltpu.VMEM((24, 128), jnp.float32)],
        compiler_params=PARAMS,
    )(goods_emb, buyer_emb, money_row)


def price_call(k, got, values, money=None):
    payload = jax.ShapeDtypeStruct((16, GT, 128), jnp.float32)
    first = k == 1
    return pl.pallas_call(
        functools.partial(price_kernel, k),
        in_specs=[VM] * (2 if first else 3),
        out_specs=[VM, VM] if first else VM,
        out_shape=[payload, jax.ShapeDtypeStruct((LB, 128), jnp.float32)] if first else payload,
        scratch_shapes=[pltpu.VMEM((LB, 128), jnp.float32), pltpu.VMEM((128, 128), jnp.float32)],
        compiler_params=PARAMS,
    )(*((got, values) if first else (got, money, values)))


def utility_call(k, got, values, before=None, zh=None):
    last = k == ITERS
    scratch = [pltpu.VMEM((GT, 128), jnp.float32), pltpu.VMEM((128, 128), jnp.float32)]
    if last:
        return pl.pallas_call(
            functools.partial(utility_kernel, k),
            in_specs=[VM, VM, pl.BlockSpec(memory_space=pltpu.SMEM), VM],
            out_specs=[VM, VM],
            out_shape=[jax.ShapeDtypeStruct((32, 5, 128), jnp.float32), jax.ShapeDtypeStruct((4, 4, 128), jnp.float32)],
            scratch_shapes=scratch,
            compiler_params=PARAMS,
        )(got, before, zh, values)
    return pl.pallas_call(
        functools.partial(utility_kernel, k),
        in_specs=[VM, VM],
        out_specs=[VM, VM],
        out_shape=[jax.ShapeDtypeStruct((32, LB, 128), jnp.float32), jax.ShapeDtypeStruct((GT, 128), jnp.float32)],
        scratch_shapes=scratch,
        compiler_params=PARAMS,
    )(got, values)


def pack_kernel(place_ref, hidden_ref, out_ref):
    x, c = place_ref[0], place_ref[2]
    rows = hidden_ref[...].T
    for q in range(8):
        to_x, to_c = q // 2, q % 2
        at = 80 * (4 * to_x + to_c)
        part = jnp.concatenate([rows[at : at + 80], rows[at + 160 : at + 240]], 1)
        out_ref[(to_c + c) & 1, (to_x + 4 - x) & 3] = part


def half_kernel(place_ref, proj_ref, *refs):
    got, (mine_ref, other_ref, weights, both) = refs[:8], refs[8:]
    x, zh, c = place_ref[0], place_ref[1], place_ref[2]
    weights[...] = jnp.zeros_like(weights)
    total = jnp.zeros((80, 2 * E), jnp.float32)
    for q in range(8):
        dx, dc = q // 2, q % 2
        w = proj_ref[((x + 4 - dx) & 3) * 4 + zh * 2 + ((c + dc) & 1)]
        weights[q, 0:64, 0:E] = w
        weights[q, 64:128, E : 2 * E] = w
        total = total + jnp.dot(got[q][...], weights[q], preferred_element_type=jnp.float32)
    both[0] = total[:, 0:E]
    both[1] = total[:, E : 2 * E]
    mine_ref[...] = both[zh]
    other_ref[...] = both[1 - zh]


def join_kernel(mine_ref, came_ref, out_ref):
    emb = (mine_ref[...] + came_ref[...]).astype(jnp.bfloat16)
    for p in range(out_ref.shape[0]):
        out_ref[p] = emb


def turn_kernel(got_ref, out_ref):
    for s in range(4):
        rows = got_ref[s].T
        for q in range(8):
            out_ref[q, :, 32 * s : 32 * s + 32] = rows[64 * q : 64 * q + 64]


def goods_kernel(got_ref, proj_ref, out_ref):
    total = jnp.dot(got_ref[0], proj_ref[0], preferred_element_type=jnp.float32)
    for q in range(1, 8):
        total = total + jnp.dot(got_ref[q], proj_ref[q], preferred_element_type=jnp.float32)
    emb = total.astype(jnp.bfloat16)
    for p in range(out_ref.shape[0]):
        out_ref[p] = emb


def small_call(kernel, outs, *args, scratch=(), smem=0):
    return pl.pallas_call(
        kernel,
        in_specs=[pl.BlockSpec(memory_space=pltpu.SMEM)] * smem + [VM] * (len(args) - smem),
        out_specs=jax.tree.map(lambda _: VM, outs),
        out_shape=outs,
        scratch_shapes=list(scratch),
        compiler_params=PARAMS,
    )(*args)


def exchange(x, axes):
    return lax.all_to_all(x, axes, 0, 0, tiled=True)


def swap(x, axis):
    return lax.ppermute(x, axis, [(0, 1), (1, 0)])


def embeddings(buyer_hidden, goods_hidden, buyer_proj, goods_proj, place):
    bf16, f32 = jnp.bfloat16, jnp.float32
    shape = jax.ShapeDtypeStruct
    goods_part = exchange(goods_hidden.T.reshape(32, 4, 512).transpose(1, 0, 2), ("y",))
    packed = small_call(pack_kernel, shape((2, 4, 80, 128), bf16), place, buyer_hidden.T, smem=1)
    here, across = packed[0], swap(packed[1], "c")
    parts = [here[0], across[0]]
    for d in range(1, 4):
        two = lax.ppermute(jnp.stack([here[d], across[d]]), "x", [(i, (i + d) % 4) for i in range(4)])
        parts += [two[0], two[1]]
    goods_rows = exchange(small_call(turn_kernel, shape((8, 64, 128), bf16), goods_part), ("zl",))
    goods_rows, parts = lax.optimization_barrier((goods_rows, parts))
    mine, other = small_call(
        half_kernel, (shape((80, E), f32),) * 2, place, buyer_proj.reshape(16, 64, E), *parts,
        scratch=(pltpu.VMEM((8, 128, 2 * E), bf16), pltpu.VMEM((2, 80, E), f32)), smem=1,
    )
    came = swap(other, "zh")
    proj = goods_proj.reshape(4, 8, 32, E).transpose(1, 0, 2, 3).reshape(8, 128, E)
    goods_emb = exchange(small_call(goods_kernel, shape((16, 64, E), bf16), goods_rows, proj), RING)
    joined = small_call(join_kernel, shape((32, 80, E), bf16), mine, came)
    joined, goods_emb = lax.optimization_barrier((joined, goods_emb))
    buyer_emb = exchange(joined, PLANE)
    return buyer_emb.reshape(-1, E), goods_emb.reshape(-1, E)


def per_device(buyer_hidden, goods_hidden, buyer_proj, goods_proj, endowment):
    x, y, zh, c = (lax.axis_index(a) for a in ("x", "y", "zh", "c"))
    place = jnp.stack([x, zh, c])
    buyer_emb, goods_emb = embeddings(buyer_hidden, goods_hidden, buyer_proj, goods_proj, place)

    mine = lax.dynamic_index_in_dim(endowment.reshape(4, 2, 160), zh, 1, keepdims=False).reshape(5, 128)
    money_row = lax.dynamic_slice(mine, (jnp.minimum(x * 2 + c, 4), 0), (1, 128))

    values, sent = values_call(goods_emb, buyer_emb, money_row)
    got = exchange(sent, PLANE)
    sent, money = price_call(1, got, values)
    for k in range(1, ITERS):
        sent, before = utility_call(k, exchange(sent, RING), values)
        got = exchange(sent, PLANE)
        sent = price_call(k + 1, got, values, money)
    sent, halves = utility_call(ITERS, exchange(sent, RING), values, before, zh.reshape(1))
    final = exchange(sent, PLANE)
    five = lambda a, axis: lax.dynamic_slice_in_dim(a, 5 * y, 5, axis)
    mine_total = jnp.sum(final, 0) * five(money, 0) / jnp.sum(five(got, 1), 0)
    other = swap(mine_total, "zh")
    prices = exchange(lax.optimization_barrier((halves, mine_total))[0], ("y",)).reshape(-1)
    first = jnp.where(zh == 0, mine_total, other).reshape(4, 160)
    second = jnp.where(zh == 0, other, mine_total).reshape(4, 160)
    utility = jnp.stack([first, second], 1).reshape(-1)
    return (prices, utility)


def solution(mesh):
    fine = Mesh(mesh.devices.reshape([n for _, n in FINE]), [a for a, _ in FINE])
    buyers, goods = ("y", "zl"), ("x", "zh", "c")
    placed = (P(buyers, goods), P(goods, buyers), P(), P(), P(buyers))
    return jax.shard_map(
        per_device, mesh=fine, in_specs=placed, out_specs=(P(goods), P(buyers)), check_vma=False
    )
```

```python
import functools

import jax
import jax.numpy as jnp
from jax import lax
from jax.experimental import pallas as pl
from jax.experimental.pallas import tpu as pltpu
from jax.sharding import Mesh, PartitionSpec as P

ITERS = 3
FINE = (("y", 4), ("zl", 8), ("x", 4), ("zh", 2), ("c", 2))
PLANE = ("y", "x", "c")
RING = ("zh", "zl")


E = 128
NBUY = 2560
NGOOD = 1024
LB = NBUY // 128
GT = NGOOD // 128


LOG2E = 1.4426950408889634
LN2 = 0.6931471805599453


def softplus_of(products):
    t = products * (E ** (-0.5) * LOG2E)
    u = jnp.exp2(jnp.minimum(t, 126.0))
    small = u * (LOG2E - (0.5 * LOG2E) * u)
    return jnp.maximum(t, jnp.where(u < 2.0**-8, small, jnp.log2(1.0 + u))) * LN2


def values_kernel(goods_ref, buyers_ref, money_ref, values_ref, out_ref, total, rows):
    step = pl.program_id(0)

    @pl.when(step == 0)
    def _():
        total[...] = jnp.zeros_like(total)

    for b in range(NBUY // 256):
        cols = slice(256 * b, 256 * b + 256)
        scores = lax.dot_general(
            goods_ref[...], buyers_ref[cols, :], (((1,), (1,)), ((), ())), preferred_element_type=jnp.float32
        )
        rounded = softplus_of(scores).astype(jnp.bfloat16)
        values_ref[:, cols] = rounded
        total[:, cols] += jnp.sum(rounded.astype(jnp.float32).reshape(-1, 8, 256), 0)

    @pl.when(step == pl.num_programs(0) - 1)
    def _():
        whole = jnp.sum(total[...], 0, keepdims=True)
        for b in range(LB):
            rows[b : b + 1, :] = whole[:, 128 * b : 128 * b + 128]
        rows[LB : LB + 1, :] = money_ref[...]
        for p in range(out_ref.shape[0]):
            out_ref[p] = rows[0 : LB + 1, :]


def powered(v, k):
    square = v * v if k >= 2 else None
    return {1: lambda: v, 2: lambda: square, 3: lambda: square * v, 4: lambda: square * square}[k]()


def price_kernel(k, got_ref, *refs):
    if k == 1:
        values, out_ref, money_ref, scale, sums = refs
        for y in range(4):
            for i in range(5):
                money_ref[5 * y + i : 5 * y + i + 1, :] = got_ref[8 * y + i, LB : LB + 1, :]
    else:
        money_ref, values, out_ref, scale, sums = refs
    total = got_ref[0, 0:LB, :]
    for p in range(1, got_ref.shape[0]):
        total = total + got_ref[p, 0:LB, :]
    scale[...] = money_ref[...] / total
    for q in range(GT):

        def chunk(i, _, q=q):
            at = pl.multiple_of(128 * q + 16 * i, 16)
            acc = None
            for b in range(LB):
                v = values[pl.ds(at, 16), 128 * b : 128 * b + 128].astype(jnp.float32)
                term = powered(v, k) * scale[b : b + 1, :]
                acc = term if acc is None else acc + term
            sums[pl.ds(pl.multiple_of(16 * i, 16), 16), :] = acc
            return 0

        lax.fori_loop(0, 8, chunk, 0, unroll=2)
        row = jnp.sum(sums[...].T, 0, keepdims=True)
        for p in range(out_ref.shape[0]):
            out_ref[p, q : q + 1, :] = row


def utility_kernel(k, got_ref, *refs):
    last = k == ITERS
    if last:
        before_ref, zh_ref, values, out_ref, prices_ref, inverse, spare = refs
    else:
        values, out_ref, sum_ref, inverse, spare = refs
    total = got_ref[0]
    for p in range(1, got_ref.shape[0]):
        total = total + got_ref[p]
    inverse[...] = 1.0 / total
    if last:
        spare[0:8, :] = total / before_ref[...]
        half = spare[pl.ds(pl.multiple_of(4 * zh_ref[0], 4), 4), :]
        for p in range(prices_ref.shape[0]):
            prices_ref[p] = half
    else:
        sum_ref[...] = total
    accs = tuple(jnp.zeros((8, 128), jnp.float32) for _ in range(LB))
    for q in range(GT):
        spare[...] = jnp.broadcast_to(inverse[q : q + 1, :], (128, 128)).T

        def chunk(i, accs, q=q):
            at = pl.multiple_of(128 * q + 16 * i, 16)
            c = spare[pl.ds(pl.multiple_of(16 * i, 16), 16), :]
            new = []
            for b in range(LB):
                v = values[pl.ds(at, 16), 128 * b : 128 * b + 128].astype(jnp.float32)
                term = powered(v, k + 1) * c
                new.append(accs[b] + (term[0:8] + term[8:16]))
            return tuple(new)

        accs = lax.fori_loop(0, 8, chunk, accs)
    for b in range(LB):
        spare[b : b + 1, :] = jnp.sum(accs[b], 0, keepdims=True)
    for p in range(out_ref.shape[0]):
        out_ref[p] = spare[5 * (p // 8) : 5 * (p // 8) + 5, :] if last else spare[0:LB, :]


VM = pl.BlockSpec(memory_space=pltpu.VMEM)
PARAMS = pltpu.CompilerParams(vmem_limit_bytes=16 << 20)


def values_call(goods_emb, buyer_emb, money_row):
    return pl.pallas_call(
        values_kernel,
        grid=(GT,),
        in_specs=[
            pl.BlockSpec((128, E), lambda i: (i, 0)),
            pl.BlockSpec((NBUY, E), lambda i: (0, 0)),
            pl.BlockSpec((1, 128), lambda i: (0, 0)),
        ],
        out_specs=[
            pl.BlockSpec((128, NBUY), lambda i: (i, 0)),
            pl.BlockSpec((32, LB + 1, 128), lambda i: (0, 0, 0)),
        ],
        out_shape=[
            jax.ShapeDtypeStruct((NGOOD, NBUY), jnp.bfloat16),
            jax.ShapeDtypeStruct((32, LB + 1, 128), jnp.float32),
        ],
        scratch_shapes=[pltpu.VMEM((8, NBUY), jnp.float32), pltpu.VMEM((24, 128), jnp.float32)],
        compiler_params=PARAMS,
    )(goods_emb, buyer_emb, money_row)


def price_call(k, got, values, money=None):
    payload = jax.ShapeDtypeStruct((16, GT, 128), jnp.float32)
    first = k == 1
    return pl.pallas_call(
        functools.partial(price_kernel, k),
        in_specs=[VM] * (2 if first else 3),
        out_specs=[VM, VM] if first else VM,
        out_shape=[payload, jax.ShapeDtypeStruct((LB, 128), jnp.float32)] if first else payload,
        scratch_shapes=[pltpu.VMEM((LB, 128), jnp.float32), pltpu.VMEM((128, 128), jnp.float32)],
        compiler_params=PARAMS,
    )(*((got, values) if first else (got, money, values)))


def utility_call(k, got, values, before=None, zh=None):
    last = k == ITERS
    scratch = [pltpu.VMEM((GT, 128), jnp.float32), pltpu.VMEM((128, 128), jnp.float32)]
    if last:
        return pl.pallas_call(
            functools.partial(utility_kernel, k),
            in_specs=[VM, VM, pl.BlockSpec(memory_space=pltpu.SMEM), VM],
            out_specs=[VM, VM],
            out_shape=[jax.ShapeDtypeStruct((32, 5, 128), jnp.float32), jax.ShapeDtypeStruct((4, 4, 128), jnp.float32)],
            scratch_shapes=scratch,
            compiler_params=PARAMS,
        )(got, before, zh, values)
    return pl.pallas_call(
        functools.partial(utility_kernel, k),
        in_specs=[VM, VM],
        out_specs=[VM, VM],
        out_shape=[jax.ShapeDtypeStruct((32, LB, 128), jnp.float32), jax.ShapeDtypeStruct((GT, 128), jnp.float32)],
        scratch_shapes=scratch,
        compiler_params=PARAMS,
    )(got, values)


def pack_kernel(place_ref, hidden_ref, out_ref):
    x, c = place_ref[0], place_ref[2]
    rows = hidden_ref[...].T
    for q in range(8):
        to_x, to_c = q // 2, q % 2
        at = 80 * (4 * to_x + to_c)
        part = jnp.concatenate([rows[at : at + 80], rows[at + 160 : at + 240]], 1)
        out_ref[(to_c + c) & 1, (to_x + 4 - x) & 3] = part


def half_kernel(place_ref, proj_ref, *refs):
    got, (mine_ref, other_ref, weights, both) = refs[:8], refs[8:]
    x, zh, c = place_ref[0], place_ref[1], place_ref[2]
    weights[...] = jnp.zeros_like(weights)
    total = jnp.zeros((80, 2 * E), jnp.float32)
    for q in range(8):
        dx, dc = q // 2, q % 2
        w = proj_ref[((x + 4 - dx) & 3) * 4 + zh * 2 + ((c + dc) & 1)]
        weights[q, 0:64, 0:E] = w
        weights[q, 64:128, E : 2 * E] = w
        total = total + jnp.dot(got[q][...], weights[q], preferred_element_type=jnp.float32)
    both[0] = total[:, 0:E]
    both[1] = total[:, E : 2 * E]
    mine_ref[...] = both[zh]
    other_ref[...] = both[1 - zh]


def join_kernel(mine_ref, came_ref, out_ref):
    emb = (mine_ref[...] + came_ref[...]).astype(jnp.bfloat16)
    for p in range(out_ref.shape[0]):
        out_ref[p] = emb


def turn_kernel(got_ref, out_ref):
    for s in range(4):
        rows = got_ref[s].T
        for q in range(8):
            out_ref[q, :, 32 * s : 32 * s + 32] = rows[64 * q : 64 * q + 64]


def goods_kernel(got_ref, proj_ref, out_ref):
    total = jnp.dot(got_ref[0], proj_ref[0], preferred_element_type=jnp.float32)
    for q in range(1, 8):
        total = total + jnp.dot(got_ref[q], proj_ref[q], preferred_element_type=jnp.float32)
    emb = total.astype(jnp.bfloat16)
    for p in range(out_ref.shape[0]):
        out_ref[p] = emb


def small_call(kernel, outs, *args, scratch=(), smem=0):
    return pl.pallas_call(
        kernel,
        in_specs=[pl.BlockSpec(memory_space=pltpu.SMEM)] * smem + [VM] * (len(args) - smem),
        out_specs=jax.tree.map(lambda _: VM, outs),
        out_shape=outs,
        scratch_shapes=list(scratch),
        compiler_params=PARAMS,
    )(*args)


def exchange(x, axes):
    return lax.all_to_all(x, axes, 0, 0, tiled=True)


def swap(x, axis):
    return lax.ppermute(x, axis, [(0, 1), (1, 0)])


def embeddings(buyer_hidden, goods_hidden, buyer_proj, goods_proj, place):
    bf16, f32 = jnp.bfloat16, jnp.float32
    shape = jax.ShapeDtypeStruct
    goods_part = exchange(goods_hidden.T.reshape(32, 4, 512).transpose(1, 0, 2), ("y",))
    packed = small_call(pack_kernel, shape((2, 4, 80, 128), bf16), place, buyer_hidden.T, smem=1)
    here, across = packed[0], swap(packed[1], "c")
    parts = [here[0], across[0]]
    for d in range(1, 4):
        two = lax.ppermute(jnp.stack([here[d], across[d]]), "x", [(i, (i + d) % 4) for i in range(4)])
        parts += [two[0], two[1]]
    goods_rows = exchange(small_call(turn_kernel, shape((8, 64, 128), bf16), goods_part), ("zl",))
    mine, other = small_call(
        half_kernel, (shape((80, E), f32),) * 2, place, buyer_proj.reshape(16, 64, E), *parts,
        scratch=(pltpu.VMEM((8, 128, 2 * E), bf16), pltpu.VMEM((2, 80, E), f32)), smem=1,
    )
    came = swap(other, "zh")
    goods_rows, _ = lax.optimization_barrier((goods_rows, other))
    proj = goods_proj.reshape(4, 8, 32, E).transpose(1, 0, 2, 3).reshape(8, 128, E)
    goods_own = small_call(goods_kernel, shape((16, 64, E), bf16), goods_rows, proj)
    goods_emb = exchange(goods_own, RING)
    joined = small_call(join_kernel, shape((32, 80, E), bf16), mine, came)
    joined, goods_emb = lax.optimization_barrier((joined, goods_emb))
    buyer_emb = exchange(joined, PLANE)
    return buyer_emb.reshape(-1, E), goods_emb.reshape(-1, E)


def per_device(buyer_hidden, goods_hidden, buyer_proj, goods_proj, endowment):
    x, y, zh, c = (lax.axis_index(a) for a in ("x", "y", "zh", "c"))
    place = jnp.stack([x, zh, c])
    buyer_emb, goods_emb = embeddings(buyer_hidden, goods_hidden, buyer_proj, goods_proj, place)

    mine = lax.dynamic_index_in_dim(endowment.reshape(4, 2, 160), zh, 1, keepdims=False).reshape(5, 128)
    money_row = lax.dynamic_slice(mine, (jnp.minimum(x * 2 + c, 4), 0), (1, 128))

    values, sent = values_call(goods_emb, buyer_emb, money_row)
    got = exchange(sent, PLANE)
    sent, money = price_call(1, got, values)
    for k in range(1, ITERS):
        sent, before = utility_call(k, exchange(sent, RING), values)
        got = exchange(sent, PLANE)
        sent = price_call(k + 1, got, values, money)
    sent, halves = utility_call(ITERS, exchange(sent, RING), values, before, zh.reshape(1))
    final = exchange(sent, PLANE)
    five = lambda a, axis: lax.dynamic_slice_in_dim(a, 5 * y, 5, axis)
    mine_total = jnp.sum(final, 0) * five(money, 0) / jnp.sum(five(got, 1), 0)
    other = swap(mine_total, "zh")
    prices = exchange(lax.optimization_barrier((halves, mine_total))[0], ("y",)).reshape(-1)
    first = jnp.where(zh == 0, mine_total, other).reshape(4, 160)
    second = jnp.where(zh == 0, other, mine_total).reshape(4, 160)
    utility = jnp.stack([first, second], 1).reshape(-1)
    return (prices, utility)


def solution(mesh):
    fine = Mesh(mesh.devices.reshape([n for _, n in FINE]), [a for a, _ in FINE])
    buyers, goods = ("y", "zl"), ("x", "zh", "c")
    placed = (P(buyers, goods), P(goods, buyers), P(), P(), P(buyers))
    return jax.shard_map(
        per_device, mesh=fine, in_specs=placed, out_specs=(P(goods), P(buyers)), check_vma=False
    )
```

```python
import functools

import jax
import jax.numpy as jnp
from jax import lax
from jax.experimental import pallas as pl
from jax.experimental.pallas import tpu as pltpu
from jax.sharding import Mesh, PartitionSpec as P

ITERS = 3
FINE = (("y", 4), ("zl", 8), ("x", 4), ("zh", 2), ("c", 2))
PLANE = ("y", "x", "c")
RING = ("zh", "zl")


E = 128
NBUY = 2560
NGOOD = 1024
LB = NBUY // 128
GT = NGOOD // 128


LOG2E = 1.4426950408889634
LN2 = 0.6931471805599453


def softplus_of(products):
    t = products * (E ** (-0.5) * LOG2E)
    u = jnp.exp2(jnp.minimum(t, 126.0))
    small = u * (LOG2E - (0.5 * LOG2E) * u)
    return jnp.maximum(t, jnp.where(u < 2.0**-8, small, jnp.log2(1.0 + u))) * LN2


def values_kernel(goods_ref, buyers_ref, money_ref, values_ref, out_ref, total, rows):
    step = pl.program_id(0)

    @pl.when(step == 0)
    def _():
        total[...] = jnp.zeros_like(total)

    for b in range(NBUY // 256):
        cols = slice(256 * b, 256 * b + 256)
        scores = lax.dot_general(
            goods_ref[...], buyers_ref[cols, :], (((1,), (1,)), ((), ())), preferred_element_type=jnp.float32
        )
        rounded = softplus_of(scores).astype(jnp.bfloat16)
        values_ref[:, cols] = rounded
        total[:, cols] += jnp.sum(rounded.astype(jnp.float32).reshape(-1, 8, 256), 0)

    @pl.when(step == pl.num_programs(0) - 1)
    def _():
        whole = jnp.sum(total[...], 0, keepdims=True)
        for b in range(LB):
            rows[b : b + 1, :] = whole[:, 128 * b : 128 * b + 128]
        rows[LB : LB + 1, :] = money_ref[...]
        for p in range(out_ref.shape[0]):
            out_ref[p] = rows[0 : LB + 1, :]


def powered(v, k):
    square = v * v if k >= 2 else None
    return {1: lambda: v, 2: lambda: square, 3: lambda: square * v, 4: lambda: square * square}[k]()


def price_kernel(k, got_ref, *refs):
    if k == 1:
        values, out_ref, money_ref, scale, sums = refs
        for y in range(4):
            for i in range(5):
                money_ref[5 * y + i : 5 * y + i + 1, :] = got_ref[8 * y + i, LB : LB + 1, :]
    else:
        money_ref, values, out_ref, scale, sums = refs
    total = got_ref[0, 0:LB, :]
    for p in range(1, got_ref.shape[0]):
        total = total + got_ref[p, 0:LB, :]
    scale[...] = money_ref[...] / total
    for q in range(GT):

        def chunk(i, _, q=q):
            at = pl.multiple_of(128 * q + 16 * i, 16)
            acc = None
            for b in range(LB):
                v = values[pl.ds(at, 16), 128 * b : 128 * b + 128].astype(jnp.float32)
                term = powered(v, k) * scale[b : b + 1, :]
                acc = term if acc is None else acc + term
            sums[pl.ds(pl.multiple_of(16 * i, 16), 16), :] = acc
            return 0

        lax.fori_loop(0, 8, chunk, 0, unroll=2)
        row = jnp.sum(sums[...].T, 0, keepdims=True)
        for p in range(out_ref.shape[0]):
            out_ref[p, q : q + 1, :] = row


def utility_kernel(k, got_ref, *refs):
    last = k == ITERS
    if last:
        before_ref, zh_ref, values, out_ref, prices_ref, inverse, spare = refs
    else:
        values, out_ref, sum_ref, inverse, spare = refs
    total = got_ref[0]
    for p in range(1, got_ref.shape[0]):
        total = total + got_ref[p]
    inverse[...] = 1.0 / total
    if last:
        spare[0:8, :] = total / before_ref[...]
        half = spare[pl.ds(pl.multiple_of(4 * zh_ref[0], 4), 4), :]
        for p in range(prices_ref.shape[0]):
            prices_ref[p] = half
    else:
        sum_ref[...] = total
    accs = tuple(jnp.zeros((8, 128), jnp.float32) for _ in range(LB))
    for q in range(GT):
        spare[...] = jnp.broadcast_to(inverse[q : q + 1, :], (128, 128)).T

        def chunk(i, accs, q=q):
            at = pl.multiple_of(128 * q + 16 * i, 16)
            c = spare[pl.ds(pl.multiple_of(16 * i, 16), 16), :]
            new = []
            for b in range(LB):
                v = values[pl.ds(at, 16), 128 * b : 128 * b + 128].astype(jnp.float32)
                term = powered(v, k + 1) * c
                new.append(accs[b] + (term[0:8] + term[8:16]))
            return tuple(new)

        accs = lax.fori_loop(0, 8, chunk, accs)
    for b in range(LB):
        spare[b : b + 1, :] = jnp.sum(accs[b], 0, keepdims=True)
    for p in range(out_ref.shape[0]):
        out_ref[p] = spare[5 * (p // 8) : 5 * (p // 8) + 5, :] if last else spare[0:LB, :]


VM = pl.BlockSpec(memory_space=pltpu.VMEM)
PARAMS = pltpu.CompilerParams(vmem_limit_bytes=16 << 20)


def values_call(goods_emb, buyer_emb, money_row):
    return pl.pallas_call(
        values_kernel,
        grid=(GT,),
        in_specs=[
            pl.BlockSpec((128, E), lambda i: (i, 0)),
            pl.BlockSpec((NBUY, E), lambda i: (0, 0)),
            pl.BlockSpec((1, 128), lambda i: (0, 0)),
        ],
        out_specs=[
            pl.BlockSpec((128, NBUY), lambda i: (i, 0)),
            pl.BlockSpec((32, LB + 1, 128), lambda i: (0, 0, 0)),
        ],
        out_shape=[
            jax.ShapeDtypeStruct((NGOOD, NBUY), jnp.bfloat16),
            jax.ShapeDtypeStruct((32, LB + 1, 128), jnp.float32),
        ],
        scratch_shapes=[pltpu.VMEM((8, NBUY), jnp.float32), pltpu.VMEM((24, 128), jnp.float32)],
        compiler_params=PARAMS,
    )(goods_emb, buyer_emb, money_row)


def price_call(k, got, values, money=None):
    payload = jax.ShapeDtypeStruct((16, GT, 128), jnp.float32)
    first = k == 1
    return pl.pallas_call(
        functools.partial(price_kernel, k),
        in_specs=[VM] * (2 if first else 3),
        out_specs=[VM, VM] if first else VM,
        out_shape=[payload, jax.ShapeDtypeStruct((LB, 128), jnp.float32)] if first else payload,
        scratch_shapes=[pltpu.VMEM((LB, 128), jnp.float32), pltpu.VMEM((128, 128), jnp.float32)],
        compiler_params=PARAMS,
    )(*((got, values) if first else (got, money, values)))


def utility_call(k, got, values, before=None, zh=None):
    last = k == ITERS
    scratch = [pltpu.VMEM((GT, 128), jnp.float32), pltpu.VMEM((128, 128), jnp.float32)]
    if last:
        return pl.pallas_call(
            functools.partial(utility_kernel, k),
            in_specs=[VM, VM, pl.BlockSpec(memory_space=pltpu.SMEM), VM],
            out_specs=[VM, VM],
            out_shape=[jax.ShapeDtypeStruct((32, 5, 128), jnp.float32), jax.ShapeDtypeStruct((4, 4, 128), jnp.float32)],
            scratch_shapes=scratch,
            compiler_params=PARAMS,
        )(got, before, zh, values)
    return pl.pallas_call(
        functools.partial(utility_kernel, k),
        in_specs=[VM, VM],
        out_specs=[VM, VM],
        out_shape=[jax.ShapeDtypeStruct((32, LB, 128), jnp.float32), jax.ShapeDtypeStruct((GT, 128), jnp.float32)],
        scratch_shapes=scratch,
        compiler_params=PARAMS,
    )(got, values)


def pack_kernel(place_ref, hidden_ref, keep_ref, go_ref):
    x, zh, c = place_ref[0], place_ref[1], place_ref[2]
    rows = hidden_ref[...].astype(jnp.float32).T

    def of(to_x, to_zh, to_c):
        at = 80 * (4 * to_x + 2 * to_zh + to_c)
        return rows[at : at + 80]

    for to_x in range(4):
        for to_zh in range(2):
            plain = jnp.concatenate([of(to_x, to_zh, 0), of(to_x, to_zh, 1)], 1)
            turned = jnp.concatenate([of(to_x, to_zh, 1), of(to_x, to_zh, 0)], 1)
            part = jnp.where(c == 0, plain, turned).astype(jnp.bfloat16)
            at = (to_x + 4 - x) & 3

            @pl.when(zh == to_zh)
            def _(at=at, part=part):
                keep_ref[at] = part

            @pl.when(zh != to_zh)
            def _(at=at, part=part):
                go_ref[at] = part


def pair_kernel(mine_ref, came_ref, here_ref, across_ref):
    for d in range(4):
        mine, came = mine_ref[d].astype(jnp.float32), came_ref[d].astype(jnp.float32)
        here_ref[d] = jnp.concatenate([mine[:, 0:64], came[:, 0:64]], 1).astype(jnp.bfloat16)
        across_ref[d] = jnp.concatenate([mine[:, 64:128], came[:, 64:128]], 1).astype(jnp.bfloat16)


def buyers_kernel(place_ref, proj_ref, *refs):
    got, (out_ref, weights) = refs[:8], refs[8:]
    x, zh, c = place_ref[0], place_ref[1], place_ref[2]
    total = jnp.zeros((80, E), jnp.float32)
    for q in range(8):
        at = ((x + 4 - q // 2) & 3) * 4 + ((c + q % 2) & 1)
        weights[q, 0:64] = proj_ref[at + 2 * zh]
        weights[q, 64:128] = proj_ref[at + 2 - 2 * zh]
        total = total + jnp.dot(got[q][...], weights[q], preferred_element_type=jnp.float32)
    emb = total.astype(jnp.bfloat16)
    for p in range(out_ref.shape[0]):
        out_ref[p] = emb


def turn_kernel(got_ref, out_ref):
    for s in range(4):
        rows = got_ref[s].T
        for q in range(8):
            out_ref[q, :, 32 * s : 32 * s + 32] = rows[64 * q : 64 * q + 64]


def goods_kernel(got_ref, proj_ref, out_ref):
    total = jnp.dot(got_ref[0], proj_ref[0], preferred_element_type=jnp.float32)
    for q in range(1, 8):
        total = total + jnp.dot(got_ref[q], proj_ref[q], preferred_element_type=jnp.float32)
    emb = total.astype(jnp.bfloat16)
    for p in range(out_ref.shape[0]):
        out_ref[p] = emb


def small_call(kernel, outs, *args, scratch=(), smem=0):
    return pl.pallas_call(
        kernel,
        in_specs=[pl.BlockSpec(memory_space=pltpu.SMEM)] * smem + [VM] * (len(args) - smem),
        out_specs=jax.tree.map(lambda _: VM, outs),
        out_shape=outs,
        scratch_shapes=list(scratch),
        compiler_params=PARAMS,
    )(*args)


def exchange(x, axes):
    return lax.all_to_all(x, axes, 0, 0, tiled=True)


def swap(x, axis):
    return lax.ppermute(x, axis, [(0, 1), (1, 0)])


def embeddings(buyer_hidden, goods_hidden, buyer_proj, goods_proj, place):
    bf16 = jnp.bfloat16
    shape = jax.ShapeDtypeStruct
    goods_part = exchange(goods_hidden.T.reshape(32, 4, 512).transpose(1, 0, 2), ("y",))
    keep, go = small_call(pack_kernel, (shape((4, 80, 128), bf16),) * 2, place, buyer_hidden.T, smem=1)
    came = swap(go, "zh")
    here, across = small_call(pair_kernel, (shape((4, 80, 128), bf16),) * 2, keep, came)
    across = swap(across, "c")
    parts = [here[0], across[0]]
    for d in range(1, 4):
        two = jnp.stack([here[d], across[d]])
        two = lax.ppermute(two, "x", [(i, (i + d) % 4) for i in range(4)])
        parts += [two[0], two[1]]
    goods_rows = exchange(small_call(turn_kernel, shape((8, 64, 128), bf16), goods_part), ("zl",))
    proj = goods_proj.reshape(4, 8, 32, E).transpose(1, 0, 2, 3).reshape(8, 128, E)
    goods_own = small_call(goods_kernel, shape((16, 64, E), bf16), goods_rows, proj)
    goods_emb = exchange(goods_own, RING)
    buyer_own = small_call(
        buyers_kernel, shape((32, 80, E), bf16), place, buyer_proj.reshape(16, 64, E), *parts,
        scratch=(pltpu.VMEM((8, 128, E), bf16),), smem=1,
    )
    buyer_own, goods_emb = lax.optimization_barrier((buyer_own, goods_emb))
    buyer_emb = exchange(buyer_own, PLANE)
    return buyer_emb.reshape(-1, E), goods_emb.reshape(-1, E)


def per_device(buyer_hidden, goods_hidden, buyer_proj, goods_proj, endowment):
    x, y, zh, c = (lax.axis_index(a) for a in ("x", "y", "zh", "c"))
    place = jnp.stack([x, zh, c])
    buyer_emb, goods_emb = embeddings(buyer_hidden, goods_hidden, buyer_proj, goods_proj, place)

    mine = lax.dynamic_index_in_dim(endowment.reshape(4, 2, 160), zh, 1, keepdims=False).reshape(5, 128)
    money_row = lax.dynamic_slice(mine, (jnp.minimum(x * 2 + c, 4), 0), (1, 128))

    values, sent = values_call(goods_emb, buyer_emb, money_row)
    got = exchange(sent, PLANE)
    sent, money = price_call(1, got, values)
    for k in range(1, ITERS):
        sent, before = utility_call(k, exchange(sent, RING), values)
        got = exchange(sent, PLANE)
        sent = price_call(k + 1, got, values, money)
    sent, halves = utility_call(ITERS, exchange(sent, RING), values, before, zh.reshape(1))
    final = exchange(sent, PLANE)
    five = lambda a, axis: lax.dynamic_slice_in_dim(a, 5 * y, 5, axis)
    mine_total = jnp.sum(final, 0) * five(money, 0) / jnp.sum(five(got, 1), 0)
    other = swap(mine_total, "zh")
    prices = exchange(lax.optimization_barrier((halves, mine_total))[0], ("y",)).reshape(-1)
    first = jnp.where(zh == 0, mine_total, other).reshape(4, 160)
    second = jnp.where(zh == 0, other, mine_total).reshape(4, 160)
    utility = jnp.stack([first, second], 1).reshape(-1)
    return (prices, utility)


def solution(mesh):
    fine = Mesh(mesh.devices.reshape([n for _, n in FINE]), [a for a, _ in FINE])
    buyers, goods = ("y", "zl"), ("x", "zh", "c")
    placed = (P(buyers, goods), P(goods, buyers), P(), P(), P(buyers))
    return jax.shard_map(
        per_device, mesh=fine, in_specs=placed, out_specs=(P(goods), P(buyers)), check_vma=False
    )
```

```python
import functools

import jax
import jax.numpy as jnp
from jax import lax
from jax.experimental import pallas as pl
from jax.experimental.pallas import tpu as pltpu
from jax.sharding import Mesh, PartitionSpec as P

ITERS = 3
FINE = (("y", 4), ("zl", 8), ("x", 4), ("zh", 2), ("c", 2))
PLANE = ("y", "x", "c")
RING = ("zh", "zl")


E = 128
NBUY = 2560
NGOOD = 1024
LB = NBUY // 128
GT = NGOOD // 128


LOG2E = 1.4426950408889634
LN2 = 0.6931471805599453


def softplus_of(products):
    t = products * (E ** (-0.5) * LOG2E)
    u = jnp.exp2(jnp.minimum(t, 126.0))
    small = u * (LOG2E - (0.5 * LOG2E) * u)
    return jnp.maximum(t, jnp.where(u < 2.0**-8, small, jnp.log2(1.0 + u))) * LN2


def values_kernel(goods_ref, buyers_ref, money_ref, values_ref, out_ref, total, rows):
    step = pl.program_id(0)

    @pl.when(step == 0)
    def _():
        total[...] = jnp.zeros_like(total)

    for b in range(NBUY // 256):
        cols = slice(256 * b, 256 * b + 256)
        scores = lax.dot_general(
            goods_ref[...], buyers_ref[cols, :], (((1,), (1,)), ((), ())), preferred_element_type=jnp.float32
        )
        rounded = softplus_of(scores).astype(jnp.bfloat16)
        values_ref[:, cols] = rounded
        total[:, cols] += jnp.sum(rounded.astype(jnp.float32).reshape(-1, 8, 256), 0)

    @pl.when(step == pl.num_programs(0) - 1)
    def _():
        whole = jnp.sum(total[...], 0, keepdims=True)
        for b in range(LB):
            rows[b : b + 1, :] = whole[:, 128 * b : 128 * b + 128]
        rows[LB : LB + 1, :] = money_ref[...]
        for p in range(out_ref.shape[0]):
            out_ref[p] = rows[0 : LB + 1, :]


def three_parts(x, lhs):
    lhs[...] = jnp.zeros_like(lhs)
    for i in range(3):
        part = x.astype(jnp.bfloat16).astype(jnp.float32)
        x = x - part
        for b in range(part.shape[0]):
            lhs[i : i + 1, 128 * b : 128 * b + 128] = part[b : b + 1, :]


def price_kernel(k, got_ref, *refs):
    if k == 1:
        values, out_ref, money_ref, lhs = refs
        for y in range(4):
            for i in range(5):
                money_ref[5 * y + i : 5 * y + i + 1, :] = got_ref[8 * y + i, LB : LB + 1, :]
    else:
        money_ref, power, out_ref, scale, sums = refs
    total = got_ref[0, 0:LB, :]
    for p in range(1, got_ref.shape[0]):
        total = total + got_ref[p, 0:LB, :]
    if k == 1:
        three_parts(money_ref[...] / total, lhs)
        products = lax.dot_general(
            lhs[...].astype(jnp.bfloat16), values[...], (((1,), (1,)), ((), ())), preferred_element_type=jnp.float32
        )
        whole = jnp.sum(products, 0, keepdims=True)
        rows = [whole[:, 128 * q : 128 * q + 128] for q in range(GT)]
    else:
        scale[...] = money_ref[...] / total

        def chunk(i, _):
            at = pl.ds(pl.multiple_of(16 * i, 16), 16)
            even = power[at, 0:128] * scale[0:1, :]
            odd = power[at, 128:256] * scale[1:2, :]
            for b in range(2, LB, 2):
                even = even + power[at, 128 * b : 128 * b + 128] * scale[b : b + 1, :]
                odd = odd + power[at, 128 * b + 128 : 128 * b + 256] * scale[b + 1 : b + 2, :]
            sums[at, :] = even + odd
            return 0

        lax.fori_loop(0, NGOOD // 16, chunk, 0, unroll=4)
        rows = [jnp.sum(sums[128 * q : 128 * q + 128, :].T, 0, keepdims=True) for q in range(GT)]
    for q in range(GT):
        for p in range(out_ref.shape[0]):
            out_ref[p, q : q + 1, :] = rows[q]


def utility_kernel(k, got_ref, *refs):
    if k == 1:
        values, out_ref, sum_ref, power, inverse, rows = refs
    elif k == 2:
        values, square, out_ref, sum_ref, power, inverse, rows = refs
    else:
        before_ref, zh_ref, square, out_ref, prices_ref, inverse, rows = refs
    total = got_ref[0]
    for p in range(1, got_ref.shape[0]):
        total = total + got_ref[p]
    if k == ITERS:
        rows[0:8, :] = total / before_ref[...]
        half = rows[pl.ds(pl.multiple_of(4 * zh_ref[0], 4), 4), :]
        for p in range(prices_ref.shape[0]):
            prices_ref[p] = half
    else:
        sum_ref[...] = total
    ratio = 1.0 / total
    for q in range(GT):
        inverse[128 * q : 128 * q + 128, :] = jnp.broadcast_to(ratio[q : q + 1, :], (128, 128)).T

    def chunk(i, accs):
        at = pl.ds(pl.multiple_of(16 * i, 16), 16)
        c = inverse[at, :]
        new = []
        for b in range(LB):
            cols = slice(128 * b, 128 * b + 128)
            if k == 1:
                v = values[at, cols].astype(jnp.float32)
                raised = v * v
            elif k == 2:
                raised = square[at, cols] * values[at, cols].astype(jnp.float32)
            else:
                v = square[at, cols]
                raised = v * v
            if k < ITERS:
                power[at, cols] = raised
            term = raised * c
            new.append(accs[b] + (term[0:8] + term[8:16]))
        return tuple(new)

    accs = tuple(jnp.zeros((8, 128), jnp.float32) for _ in range(LB))
    accs = lax.fori_loop(0, NGOOD // 16, chunk, accs, unroll=2)
    for b in range(LB):
        rows[b : b + 1, :] = jnp.sum(accs[b], 0, keepdims=True)
    for p in range(out_ref.shape[0]):
        out_ref[p] = rows[5 * (p // 8) : 5 * (p // 8) + 5, :] if k == ITERS else rows[0:LB, :]


VM = pl.BlockSpec(memory_space=pltpu.VMEM)
PARAMS = pltpu.CompilerParams(vmem_limit_bytes=16 << 20)


def values_call(goods_emb, buyer_emb, money_row):
    return pl.pallas_call(
        values_kernel,
        grid=(GT,),
        in_specs=[
            pl.BlockSpec((128, E), lambda i: (i, 0)),
            pl.BlockSpec((NBUY, E), lambda i: (0, 0)),
            pl.BlockSpec((1, 128), lambda i: (0, 0)),
        ],
        out_specs=[
            pl.BlockSpec((128, NBUY), lambda i: (i, 0)),
            pl.BlockSpec((32, LB + 1, 128), lambda i: (0, 0, 0)),
        ],
        out_shape=[
            jax.ShapeDtypeStruct((NGOOD, NBUY), jnp.bfloat16),
            jax.ShapeDtypeStruct((32, LB + 1, 128), jnp.float32),
        ],
        scratch_shapes=[pltpu.VMEM((8, NBUY), jnp.float32), pltpu.VMEM((24, 128), jnp.float32)],
        compiler_params=PARAMS,
    )(goods_emb, buyer_emb, money_row)


def price_call(k, got, power, money=None):
    payload = jax.ShapeDtypeStruct((16, GT, 128), jnp.float32)
    first = k == 1
    scratch = [(8, NBUY)] if first else [(LB, 128), (NGOOD, 128)]
    return pl.pallas_call(
        functools.partial(price_kernel, k),
        in_specs=[VM] * (2 if first else 3),
        out_specs=[VM, VM] if first else VM,
        out_shape=[payload, jax.ShapeDtypeStruct((LB, 128), jnp.float32)] if first else payload,
        scratch_shapes=[pltpu.VMEM(x, jnp.float32) for x in scratch],
        compiler_params=PARAMS,
    )(*((got, power) if first else (got, money, power)))


def utility_call(k, got, *blocks):
    if k == ITERS:
        outs, specs = [(32, 5, 128), (4, 4, 128)], [VM, VM, pl.BlockSpec(memory_space=pltpu.SMEM), VM]
    else:
        outs, specs = [(32, LB, 128), (GT, 128), (NGOOD, NBUY)], [VM] * (1 + len(blocks))
    return pl.pallas_call(
        functools.partial(utility_kernel, k),
        in_specs=specs,
        out_specs=[VM] * len(outs),
        out_shape=[jax.ShapeDtypeStruct(o, jnp.float32) for o in outs],
        scratch_shapes=[pltpu.VMEM((NGOOD, 128), jnp.float32), pltpu.VMEM((24, 128), jnp.float32)],
        compiler_params=PARAMS,
    )(got, *blocks)


def pack_kernel(place_ref, hidden_ref, keep_ref, go_ref):
    x, zh, c = place_ref[0], place_ref[1], place_ref[2]
    rows = hidden_ref[...].astype(jnp.float32).T

    def of(to_x, to_zh, to_c):
        at = 80 * (4 * to_x + 2 * to_zh + to_c)
        return rows[at : at + 80]

    for to_x in range(4):
        for to_zh in range(2):
            plain = jnp.concatenate([of(to_x, to_zh, 0), of(to_x, to_zh, 1)], 1)
            turned = jnp.concatenate([of(to_x, to_zh, 1), of(to_x, to_zh, 0)], 1)
            part = jnp.where(c == 0, plain, turned).astype(jnp.bfloat16)
            at = (to_x + 4 - x) & 3

            @pl.when(zh == to_zh)
            def _(at=at, part=part):
                keep_ref[at] = part

            @pl.when(zh != to_zh)
            def _(at=at, part=part):
                go_ref[at] = part


def pair_kernel(mine_ref, came_ref, here_ref, across_ref):
    for d in range(4):
        mine, came = mine_ref[d].astype(jnp.float32), came_ref[d].astype(jnp.float32)
        here_ref[d] = jnp.concatenate([mine[:, 0:64], came[:, 0:64]], 1).astype(jnp.bfloat16)
        across_ref[d] = jnp.concatenate([mine[:, 64:128], came[:, 64:128]], 1).astype(jnp.bfloat16)


def buyers_kernel(place_ref, proj_ref, *refs):
    got, (out_ref, weights) = refs[:8], refs[8:]
    x, zh, c = place_ref[0], place_ref[1], place_ref[2]
    total = jnp.zeros((80, E), jnp.float32)
    for q in range(8):
        at = ((x + 4 - q // 2) & 3) * 4 + ((c + q % 2) & 1)
        weights[q, 0:64] = proj_ref[at + 2 * zh]
        weights[q, 64:128] = proj_ref[at + 2 - 2 * zh]
        total = total + jnp.dot(got[q][...], weights[q], preferred_element_type=jnp.float32)
    emb = total.astype(jnp.bfloat16)
    for p in range(out_ref.shape[0]):
        out_ref[p] = emb


def turn_kernel(got_ref, out_ref):
    for s in range(4):
        rows = got_ref[s].T
        for q in range(8):
            out_ref[q, :, 32 * s : 32 * s + 32] = rows[64 * q : 64 * q + 64]


def goods_kernel(got_ref, proj_ref, out_ref):
    total = jnp.dot(got_ref[0], proj_ref[0], preferred_element_type=jnp.float32)
    for q in range(1, 8):
        total = total + jnp.dot(got_ref[q], proj_ref[q], preferred_element_type=jnp.float32)
    emb = total.astype(jnp.bfloat16)
    for p in range(out_ref.shape[0]):
        out_ref[p] = emb


def small_call(kernel, outs, *args, scratch=(), smem=0):
    return pl.pallas_call(
        kernel,
        in_specs=[pl.BlockSpec(memory_space=pltpu.SMEM)] * smem + [VM] * (len(args) - smem),
        out_specs=jax.tree.map(lambda _: VM, outs),
        out_shape=outs,
        scratch_shapes=list(scratch),
        compiler_params=PARAMS,
    )(*args)


def exchange(x, axes):
    return lax.all_to_all(x, axes, 0, 0, tiled=True)


def swap(x, axis):
    return lax.ppermute(x, axis, [(0, 1), (1, 0)])


def embeddings(buyer_hidden, goods_hidden, buyer_proj, goods_proj, place):
    bf16 = jnp.bfloat16
    shape = jax.ShapeDtypeStruct
    goods_part = exchange(goods_hidden.T.reshape(32, 4, 512).transpose(1, 0, 2), ("y",))
    keep, go = small_call(pack_kernel, (shape((4, 80, 128), bf16),) * 2, place, buyer_hidden.T, smem=1)
    came = swap(go, "zh")
    here, across = small_call(pair_kernel, (shape((4, 80, 128), bf16),) * 2, keep, came)
    across = swap(across, "c")
    parts = [here[0], across[0]]
    for d in range(1, 4):
        two = jnp.stack([here[d], across[d]])
        two = lax.ppermute(two, "x", [(i, (i + d) % 4) for i in range(4)])
        parts += [two[0], two[1]]
    goods_rows = exchange(small_call(turn_kernel, shape((8, 64, 128), bf16), goods_part), ("zl",))
    proj = goods_proj.reshape(4, 8, 32, E).transpose(1, 0, 2, 3).reshape(8, 128, E)
    goods_own = small_call(goods_kernel, shape((16, 64, E), bf16), goods_rows, proj)
    goods_emb = exchange(goods_own, RING)
    buyer_own = small_call(
        buyers_kernel, shape((32, 80, E), bf16), place, buyer_proj.reshape(16, 64, E), *parts,
        scratch=(pltpu.VMEM((8, 128, E), bf16),), smem=1,
    )
    buyer_own, goods_emb = lax.optimization_barrier((buyer_own, goods_emb))
    buyer_emb = exchange(buyer_own, PLANE)
    return buyer_emb.reshape(-1, E), goods_emb.reshape(-1, E)


def per_device(buyer_hidden, goods_hidden, buyer_proj, goods_proj, endowment):
    x, y, zh, c = (lax.axis_index(a) for a in ("x", "y", "zh", "c"))
    place = jnp.stack([x, zh, c])
    buyer_emb, goods_emb = embeddings(buyer_hidden, goods_hidden, buyer_proj, goods_proj, place)

    mine = lax.dynamic_index_in_dim(endowment.reshape(4, 2, 160), zh, 1, keepdims=False).reshape(5, 128)
    money_row = lax.dynamic_slice(mine, (jnp.minimum(x * 2 + c, 4), 0), (1, 128))

    values, sent = values_call(goods_emb, buyer_emb, money_row)
    got = exchange(sent, PLANE)
    sent, money = price_call(1, got, values)
    sent, _, square = utility_call(1, exchange(sent, RING), values)
    sent = price_call(2, exchange(sent, PLANE), square, money)
    sent, before, cube = utility_call(2, exchange(sent, RING), values, square)
    got = exchange(sent, PLANE)
    sent = price_call(3, got, cube, money)
    sent, halves = utility_call(3, exchange(sent, RING), before, zh.reshape(1), square)
    final = exchange(sent, PLANE)
    five = lambda a, axis: lax.dynamic_slice_in_dim(a, 5 * y, 5, axis)
    mine_total = jnp.sum(final, 0) * five(money, 0) / jnp.sum(five(got, 1), 0)
    other = swap(mine_total, "zh")
    prices = exchange(lax.optimization_barrier((halves, mine_total))[0], ("y",)).reshape(-1)
    first = jnp.where(zh == 0, mine_total, other).reshape(4, 160)
    second = jnp.where(zh == 0, other, mine_total).reshape(4, 160)
    utility = jnp.stack([first, second], 1).reshape(-1)
    return (prices, utility)


def solution(mesh):
    fine = Mesh(mesh.devices.reshape([n for _, n in FINE]), [a for a, _ in FINE])
    buyers, goods = ("y", "zl"), ("x", "zh", "c")
    placed = (P(buyers, goods), P(goods, buyers), P(), P(), P(buyers))
    return jax.shard_map(
        per_device, mesh=fine, in_specs=placed, out_specs=(P(goods), P(buyers)), check_vma=False
    )
```

```python
import functools

import jax
import jax.numpy as jnp
from jax import lax
from jax.experimental import pallas as pl
from jax.experimental.pallas import tpu as pltpu
from jax.sharding import Mesh, PartitionSpec as P

ITERS = 3
FINE = (("y", 4), ("zl", 8), ("x", 4), ("zh", 2), ("c", 2))
PLANE = ("y", "x", "c")
RING = ("zh", "zl")


E = 128
NBUY = 2560
NGOOD = 1024
LB = NBUY // 128
GT = NGOOD // 128


LOG2E = 1.4426950408889634
LN2 = 0.6931471805599453


def softplus_of(products):
    t = products * (E ** (-0.5) * LOG2E)
    u = jnp.exp2(jnp.minimum(t, 126.0))
    small = u * (LOG2E - (0.5 * LOG2E) * u)
    return jnp.maximum(t, jnp.where(u < 2.0**-8, small, jnp.log2(1.0 + u))) * LN2


def values_kernel(goods_ref, buyers_ref, money_ref, values_ref, out_ref, total, rows):
    step = pl.program_id(0)

    @pl.when(step == 0)
    def _():
        total[...] = jnp.zeros_like(total)

    for b in range(NBUY // 256):
        cols = slice(256 * b, 256 * b + 256)
        scores = lax.dot_general(
            goods_ref[...], buyers_ref[cols, :], (((1,), (1,)), ((), ())), preferred_element_type=jnp.float32
        )
        rounded = softplus_of(scores).astype(jnp.bfloat16)
        values_ref[:, cols] = rounded
        total[:, cols] += jnp.sum(rounded.astype(jnp.float32).reshape(-1, 8, 256), 0)

    @pl.when(step == pl.num_programs(0) - 1)
    def _():
        whole = jnp.sum(total[...], 0, keepdims=True)
        for b in range(LB):
            rows[b : b + 1, :] = whole[:, 128 * b : 128 * b + 128]
        rows[LB : LB + 1, :] = money_ref[...]
        for p in range(out_ref.shape[0]):
            out_ref[p] = rows[0 : LB + 1, :]


def three_parts(x, lhs):
    lhs[...] = jnp.zeros_like(lhs)
    for i in range(3):
        part = x.astype(jnp.bfloat16).astype(jnp.float32)
        x = x - part
        for b in range(part.shape[0]):
            lhs[i : i + 1, 128 * b : 128 * b + 128] = part[b : b + 1, :]


def price_kernel(k, got_ref, *refs):
    if k == 1:
        values, out_ref, money_ref, lhs = refs
        for y in range(4):
            for i in range(5):
                money_ref[5 * y + i : 5 * y + i + 1, :] = got_ref[8 * y + i, LB : LB + 1, :]
    else:
        money_ref, power, out_ref, scale, sums = refs
    total = got_ref[0, 0:LB, :]
    for p in range(1, got_ref.shape[0]):
        total = total + got_ref[p, 0:LB, :]
    if k == 1:
        three_parts(money_ref[...] / total, lhs)
        products = lax.dot_general(
            lhs[...].astype(jnp.bfloat16), values[...], (((1,), (1,)), ((), ())), preferred_element_type=jnp.float32
        )
        whole = jnp.sum(products, 0, keepdims=True)
        rows = [whole[:, 128 * q : 128 * q + 128] for q in range(GT)]
    else:
        scale[...] = money_ref[...] / total

        def chunk(i, _):
            at = pl.ds(pl.multiple_of(16 * i, 16), 16)
            even = power[at, 0:128] * scale[0:1, :]
            odd = power[at, 128:256] * scale[1:2, :]
            for b in range(2, LB, 2):
                even = even + power[at, 128 * b : 128 * b + 128] * scale[b : b + 1, :]
                odd = odd + power[at, 128 * b + 128 : 128 * b + 256] * scale[b + 1 : b + 2, :]
            sums[at, :] = even + odd
            return 0

        lax.fori_loop(0, NGOOD // 16, chunk, 0, unroll=4)
        rows = [jnp.sum(sums[128 * q : 128 * q + 128, :].T, 0, keepdims=True) for q in range(GT)]
    for q in range(GT):
        for p in range(out_ref.shape[0]):
            out_ref[p, q : q + 1, :] = rows[q]


def utility_kernel(k, got_ref, *refs):
    if k == 1:
        values, out_ref, sum_ref, power, inverse, rows = refs
    elif k == 2:
        values, square, out_ref, sum_ref, power, inverse, rows = refs
    else:
        before_ref, zh_ref, square, out_ref, prices_ref, inverse, rows = refs
    total = got_ref[0]
    for p in range(1, got_ref.shape[0]):
        total = total + got_ref[p]
    if k == ITERS:
        rows[0:8, :] = total / before_ref[...]
        half = rows[pl.ds(pl.multiple_of(4 * zh_ref[0], 4), 4), :]
        for p in range(prices_ref.shape[0]):
            prices_ref[p] = half
    else:
        sum_ref[...] = total
    ratio = 1.0 / total
    for q in range(GT):
        inverse[128 * q : 128 * q + 128, :] = jnp.broadcast_to(ratio[q : q + 1, :], (128, 128)).T

    def chunk(i, accs):
        at = pl.ds(pl.multiple_of(16 * i, 16), 16)
        c = inverse[at, :]
        new = []
        for b in range(LB):
            cols = slice(128 * b, 128 * b + 128)
            if k == 1:
                v = values[at, cols].astype(jnp.float32)
                raised = v * v
            elif k == 2:
                raised = square[at, cols] * values[at, cols].astype(jnp.float32)
            else:
                v = square[at, cols]
                raised = v * v
            if k < ITERS:
                power[at, cols] = raised
            term = raised * c
            new.append(accs[b] + (term[0:8] + term[8:16]))
        return tuple(new)

    accs = tuple(jnp.zeros((8, 128), jnp.float32) for _ in range(LB))
    accs = lax.fori_loop(0, NGOOD // 16, chunk, accs, unroll=2)
    for b in range(LB):
        rows[b : b + 1, :] = jnp.sum(accs[b], 0, keepdims=True)
    for p in range(out_ref.shape[0]):
        out_ref[p] = rows[5 * (p // 8) : 5 * (p // 8) + 5, :] if k == ITERS else rows[0:LB, :]


VM = pl.BlockSpec(memory_space=pltpu.VMEM)
PARAMS = pltpu.CompilerParams(vmem_limit_bytes=16 << 20)


def values_call(goods_emb, buyer_emb, money_row):
    return pl.pallas_call(
        values_kernel,
        grid=(GT,),
        in_specs=[
            pl.BlockSpec((128, E), lambda i: (i, 0)),
            pl.BlockSpec((NBUY, E), lambda i: (0, 0)),
            pl.BlockSpec((1, 128), lambda i: (0, 0)),
        ],
        out_specs=[
            pl.BlockSpec((128, NBUY), lambda i: (i, 0)),
            pl.BlockSpec((32, LB + 1, 128), lambda i: (0, 0, 0)),
        ],
        out_shape=[
            jax.ShapeDtypeStruct((NGOOD, NBUY), jnp.bfloat16),
            jax.ShapeDtypeStruct((32, LB + 1, 128), jnp.float32),
        ],
        scratch_shapes=[pltpu.VMEM((8, NBUY), jnp.float32), pltpu.VMEM((24, 128), jnp.float32)],
        compiler_params=PARAMS,
    )(goods_emb, buyer_emb, money_row)


def price_call(k, got, power, money=None):
    payload = jax.ShapeDtypeStruct((16, GT, 128), jnp.float32)
    first = k == 1
    scratch = [(8, NBUY)] if first else [(LB, 128), (NGOOD, 128)]
    return pl.pallas_call(
        functools.partial(price_kernel, k),
        in_specs=[VM] * (2 if first else 3),
        out_specs=[VM, VM] if first else VM,
        out_shape=[payload, jax.ShapeDtypeStruct((LB, 128), jnp.float32)] if first else payload,
        scratch_shapes=[pltpu.VMEM(x, jnp.float32) for x in scratch],
        compiler_params=PARAMS,
    )(*((got, power) if first else (got, money, power)))


def utility_call(k, got, *blocks):
    if k == ITERS:
        outs, specs = [(32, 5, 128), (4, 4, 128)], [VM, VM, pl.BlockSpec(memory_space=pltpu.SMEM), VM]
    else:
        outs, specs = [(32, LB, 128), (GT, 128), (NGOOD, NBUY)], [VM] * (1 + len(blocks))
    return pl.pallas_call(
        functools.partial(utility_kernel, k),
        in_specs=specs,
        out_specs=[VM] * len(outs),
        out_shape=[jax.ShapeDtypeStruct(o, jnp.float32) for o in outs],
        scratch_shapes=[pltpu.VMEM((NGOOD, 128), jnp.float32), pltpu.VMEM((24, 128), jnp.float32)],
        compiler_params=PARAMS,
    )(got, *blocks)


def pack_kernel(place_ref, hidden_ref, keep_ref, go_ref):
    x, zh, c = place_ref[0], place_ref[1], place_ref[2]
    rows = hidden_ref[...].astype(jnp.float32).T

    def of(to_x, to_zh, to_c):
        at = 80 * (4 * to_x + 2 * to_zh + to_c)
        return rows[at : at + 80]

    for to_x in range(4):
        for to_zh in range(2):
            plain = jnp.concatenate([of(to_x, to_zh, 0), of(to_x, to_zh, 1)], 1)
            turned = jnp.concatenate([of(to_x, to_zh, 1), of(to_x, to_zh, 0)], 1)
            part = jnp.where(c == 0, plain, turned).astype(jnp.bfloat16)
            at = (to_x + 4 - x) & 3

            @pl.when(zh == to_zh)
            def _(at=at, part=part):
                keep_ref[at] = part

            @pl.when(zh != to_zh)
            def _(at=at, part=part):
                go_ref[at] = part


def pair_kernel(mine_ref, came_ref, here_ref, across_ref):
    for d in range(4):
        mine, came = mine_ref[d].astype(jnp.float32), came_ref[d].astype(jnp.float32)
        here_ref[d] = jnp.concatenate([mine[:, 0:64], came[:, 0:64]], 1).astype(jnp.bfloat16)
        across_ref[d] = jnp.concatenate([mine[:, 64:128], came[:, 64:128]], 1).astype(jnp.bfloat16)


def buyers_kernel(place_ref, proj_ref, *refs):
    got, (out_ref, weights) = refs[:8], refs[8:]
    x, zh, c = place_ref[0], place_ref[1], place_ref[2]
    total = jnp.zeros((80, E), jnp.float32)
    for q in range(8):
        at = ((x + 4 - q // 2) & 3) * 4 + ((c + q % 2) & 1)
        weights[q, 0:64] = proj_ref[at + 2 * zh]
        weights[q, 64:128] = proj_ref[at + 2 - 2 * zh]
        total = total + jnp.dot(got[q][...], weights[q], preferred_element_type=jnp.float32)
    emb = total.astype(jnp.bfloat16)
    for p in range(out_ref.shape[0]):
        out_ref[p] = emb


def tiles_kernel(hidden_ref, out_ref):
    for t in range(16):
        top = hidden_ref[0:16, 128 * t : 128 * t + 128].astype(jnp.float32)
        low = hidden_ref[16:32, 128 * t : 128 * t + 128].astype(jnp.float32)
        out_ref[2 * t] = jnp.concatenate([top[:, 0:64], low[:, 0:64]], 1).astype(jnp.bfloat16)
        out_ref[2 * t + 1] = jnp.concatenate([top[:, 64:128], low[:, 64:128]], 1).astype(jnp.bfloat16)


def goods_kernel(got_ref, proj_ref, out_ref):
    hidden = got_ref[...].reshape(512, 128).astype(jnp.float32).T.astype(jnp.bfloat16)
    halves = [
        jnp.dot(hidden[64 * h : 64 * h + 64], proj_ref[:, h].reshape(512, E), preferred_element_type=jnp.float32)
        for h in range(2)
    ]
    emb = (halves[0] + halves[1]).astype(jnp.bfloat16)
    for p in range(out_ref.shape[0]):
        out_ref[p] = emb


def small_call(kernel, outs, *args, scratch=(), smem=0):
    return pl.pallas_call(
        kernel,
        in_specs=[pl.BlockSpec(memory_space=pltpu.SMEM)] * smem + [VM] * (len(args) - smem),
        out_specs=jax.tree.map(lambda _: VM, outs),
        out_shape=outs,
        scratch_shapes=list(scratch),
        compiler_params=PARAMS,
    )(*args)


def exchange(x, axes):
    return lax.all_to_all(x, axes, 0, 0, tiled=True)


def swap(x, axis):
    return lax.ppermute(x, axis, [(0, 1), (1, 0)])


def embeddings(buyer_hidden, goods_hidden, buyer_proj, goods_proj, place):
    bf16 = jnp.bfloat16
    shape = jax.ShapeDtypeStruct
    keep, go = small_call(pack_kernel, (shape((4, 80, 128), bf16),) * 2, place, buyer_hidden.T, smem=1)
    came = swap(go, "zh")
    here, across = small_call(pair_kernel, (shape((4, 80, 128), bf16),) * 2, keep, came)
    across = swap(across, "c")
    parts = [here[0], across[0]]
    for d in range(1, 4):
        two = jnp.stack([here[d], across[d]])
        two = lax.ppermute(two, "x", [(i, (i + d) % 4) for i in range(4)])
        parts += [two[0], two[1]]
    tiles = small_call(tiles_kernel, shape((32, 16, 128), bf16), goods_hidden.T)
    tiles = exchange(tiles, ("y", "zl"))
    goods_own = small_call(goods_kernel, shape((16, 64, E), bf16), tiles, goods_proj.reshape(32, 2, 16, E))
    goods_emb = exchange(goods_own, RING)
    buyer_own = small_call(
        buyers_kernel, shape((32, 80, E), bf16), place, buyer_proj.reshape(16, 64, E), *parts,
        scratch=(pltpu.VMEM((8, 128, E), bf16),), smem=1,
    )
    buyer_own, goods_emb = lax.optimization_barrier((buyer_own, goods_emb))
    buyer_emb = exchange(buyer_own, PLANE)
    return buyer_emb.reshape(-1, E), goods_emb.reshape(-1, E)


def per_device(buyer_hidden, goods_hidden, buyer_proj, goods_proj, endowment):
    x, y, zh, c = (lax.axis_index(a) for a in ("x", "y", "zh", "c"))
    place = jnp.stack([x, zh, c])
    buyer_emb, goods_emb = embeddings(buyer_hidden, goods_hidden, buyer_proj, goods_proj, place)

    mine = lax.dynamic_index_in_dim(endowment.reshape(4, 2, 160), zh, 1, keepdims=False).reshape(5, 128)
    money_row = lax.dynamic_slice(mine, (jnp.minimum(x * 2 + c, 4), 0), (1, 128))

    values, sent = values_call(goods_emb, buyer_emb, money_row)
    got = exchange(sent, PLANE)
    sent, money = price_call(1, got, values)
    sent, _, square = utility_call(1, exchange(sent, RING), values)
    sent = price_call(2, exchange(sent, PLANE), square, money)
    sent, before, cube = utility_call(2, exchange(sent, RING), values, square)
    got = exchange(sent, PLANE)
    sent = price_call(3, got, cube, money)
    sent, halves = utility_call(3, exchange(sent, RING), before, zh.reshape(1), square)
    final = exchange(sent, PLANE)
    five = lambda a, axis: lax.dynamic_slice_in_dim(a, 5 * y, 5, axis)
    mine_total = jnp.sum(final, 0) * five(money, 0) / jnp.sum(five(got, 1), 0)
    other = swap(mine_total, "zh")
    prices = exchange(lax.optimization_barrier((halves, mine_total))[0], ("y",)).reshape(-1)
    first = jnp.where(zh == 0, mine_total, other).reshape(4, 160)
    second = jnp.where(zh == 0, other, mine_total).reshape(4, 160)
    utility = jnp.stack([first, second], 1).reshape(-1)
    return (prices, utility)


def solution(mesh):
    fine = Mesh(mesh.devices.reshape([n for _, n in FINE]), [a for a, _ in FINE])
    buyers, goods = ("y", "zl"), ("x", "zh", "c")
    placed = (P(buyers, goods), P(goods, buyers), P(), P(), P(buyers))
    return jax.shard_map(
        per_device, mesh=fine, in_specs=placed, out_specs=(P(goods), P(buyers)), check_vma=False
    )
```

```python
import functools

import jax
import jax.numpy as jnp
from jax import lax
from jax.experimental import pallas as pl
from jax.experimental.pallas import tpu as pltpu
from jax.sharding import Mesh, PartitionSpec as P

ITERS = 3
FINE = (("y", 4), ("zl", 8), ("x", 4), ("zh", 2), ("c", 2))
PLANE = ("y", "x", "c")
RING = ("zh", "zl")


E = 128
NBUY = 2560
NGOOD = 1024
LB = NBUY // 128
GT = NGOOD // 128


LOG2E = 1.4426950408889634
LN2 = 0.6931471805599453


def softplus_of(products):
    t = products * (E ** (-0.5) * LOG2E)
    u = jnp.exp2(jnp.minimum(t, 126.0))
    small = u * (LOG2E - (0.5 * LOG2E) * u)
    return jnp.maximum(t, jnp.where(u < 2.0**-8, small, jnp.log2(1.0 + u))) * LN2


def values_kernel(goods_ref, buyers_ref, money_ref, values_ref, out_ref, total, rows):
    step = pl.program_id(0)

    @pl.when(step == 0)
    def _():
        total[...] = jnp.zeros_like(total)

    for b in range(NBUY // 256):
        cols = slice(256 * b, 256 * b + 256)
        scores = lax.dot_general(
            goods_ref[...], buyers_ref[cols, :], (((1,), (1,)), ((), ())), preferred_element_type=jnp.float32
        )
        rounded = softplus_of(scores).astype(jnp.bfloat16)
        values_ref[:, cols] = rounded
        total[:, cols] += jnp.sum(rounded.astype(jnp.float32).reshape(-1, 8, 256), 0)

    @pl.when(step == pl.num_programs(0) - 1)
    def _():
        whole = jnp.sum(total[...], 0, keepdims=True)
        for b in range(LB):
            rows[b : b + 1, :] = whole[:, 128 * b : 128 * b + 128]
        rows[LB : LB + 1, :] = money_ref[...]
        for p in range(out_ref.shape[0]):
            out_ref[p] = rows[0 : LB + 1, :]


def three_parts(x, lhs):
    lhs[...] = jnp.zeros_like(lhs)
    for i in range(3):
        part = x.astype(jnp.bfloat16).astype(jnp.float32)
        x = x - part
        for b in range(part.shape[0]):
            lhs[i : i + 1, 128 * b : 128 * b + 128] = part[b : b + 1, :]


def price_kernel(k, got_ref, *refs):
    if k == 1:
        values, out_ref, money_ref, lhs, money = refs
        for b in range(LB):
            row = got_ref[8 * (b // 5) + b % 5, LB : LB + 1, :]
            money[b : b + 1, :] = row
            money_ref[b // 5 : b // 5 + 1, 128 * (b % 5) : 128 * (b % 5) + 128] = row
        total = got_ref[0, 0:LB, :]
        for p in range(1, got_ref.shape[0]):
            total = total + got_ref[p, 0:LB, :]
        three_parts(money[...] / total, lhs)
        products = lax.dot_general(
            lhs[...].astype(jnp.bfloat16), values[...], (((1,), (1,)), ((), ())), preferred_element_type=jnp.float32
        )
        whole = jnp.sum(products, 0, keepdims=True)
        rows = [whole[:, 128 * q : 128 * q + 128] for q in range(GT)]
    else:
        money_ref, power, out_ref, scale, sums = refs
        total = got_ref[0]
        for p in range(1, got_ref.shape[0]):
            total = total + got_ref[p]
        scale[...] = money_ref[...] / total

        def chunk(i, _):
            at = pl.ds(pl.multiple_of(16 * i, 16), 16)
            two = [None, None]
            for b in range(LB):
                part = scale[b // 5 : b // 5 + 1, 128 * (b % 5) : 128 * (b % 5) + 128]
                term = power[at, 128 * b : 128 * b + 128] * part
                two[b % 2] = term if two[b % 2] is None else two[b % 2] + term
            sums[at, :] = two[0] + two[1]
            return 0

        lax.fori_loop(0, NGOOD // 16, chunk, 0, unroll=4)
        rows = [jnp.sum(sums[128 * q : 128 * q + 128, :].T, 0, keepdims=True) for q in range(GT)]
    for q in range(GT):
        for p in range(out_ref.shape[0]):
            out_ref[p, q : q + 1, :] = rows[q]


def utility_kernel(k, got_ref, *refs):
    if k == 1:
        values, out_ref, sum_ref, power, inverse, rows = refs
    elif k == 2:
        values, square, out_ref, sum_ref, power, inverse, rows = refs
    else:
        before_ref, zh_ref, square, out_ref, prices_ref, inverse, rows = refs
    total = got_ref[0]
    for p in range(1, got_ref.shape[0]):
        total = total + got_ref[p]
    if k == ITERS:
        rows[0:8, :] = total / before_ref[...]
        half = rows[pl.ds(pl.multiple_of(4 * zh_ref[0], 4), 4), :]
        for p in range(prices_ref.shape[0]):
            prices_ref[p] = half
    else:
        sum_ref[...] = total
    ratio = 1.0 / total
    for q in range(GT):
        inverse[128 * q : 128 * q + 128, :] = jnp.broadcast_to(ratio[q : q + 1, :], (128, 128)).T

    def chunk(i, accs):
        at = pl.ds(pl.multiple_of(16 * i, 16), 16)
        c = inverse[at, :]
        new = []
        for b in range(LB):
            cols = slice(128 * b, 128 * b + 128)
            if k == 1:
                v = values[at, cols].astype(jnp.float32)
                raised = v * v
            elif k == 2:
                raised = square[at, cols] * values[at, cols].astype(jnp.float32)
            else:
                v = square[at, cols]
                raised = v * v
            if k < ITERS:
                power[at, cols] = raised
            term = raised * c
            new.append(accs[b] + (term[0:8] + term[8:16]))
        return tuple(new)

    accs = tuple(jnp.zeros((8, 128), jnp.float32) for _ in range(LB))
    accs = lax.fori_loop(0, NGOOD // 16, chunk, accs, unroll=2)
    for b in range(LB):
        row = jnp.sum(accs[b], 0, keepdims=True)
        if k == ITERS:
            rows[b : b + 1, :] = row
        else:
            rows[b // 5 : b // 5 + 1, 128 * (b % 5) : 128 * (b % 5) + 128] = row
    for p in range(out_ref.shape[0]):
        out_ref[p] = rows[5 * (p // 8) : 5 * (p // 8) + 5, :] if k == ITERS else rows[0:4, :]


VM = pl.BlockSpec(memory_space=pltpu.VMEM)
PARAMS = pltpu.CompilerParams(vmem_limit_bytes=16 << 20)


def values_call(goods_emb, buyer_emb, money_row):
    return pl.pallas_call(
        values_kernel,
        grid=(GT,),
        in_specs=[
            pl.BlockSpec((128, E), lambda i: (i, 0)),
            pl.BlockSpec((NBUY, E), lambda i: (0, 0)),
            pl.BlockSpec((1, 128), lambda i: (0, 0)),
        ],
        out_specs=[
            pl.BlockSpec((128, NBUY), lambda i: (i, 0)),
            pl.BlockSpec((32, LB + 1, 128), lambda i: (0, 0, 0)),
        ],
        out_shape=[
            jax.ShapeDtypeStruct((NGOOD, NBUY), jnp.bfloat16),
            jax.ShapeDtypeStruct((32, LB + 1, 128), jnp.float32),
        ],
        scratch_shapes=[pltpu.VMEM((8, NBUY), jnp.float32), pltpu.VMEM((24, 128), jnp.float32)],
        compiler_params=PARAMS,
    )(goods_emb, buyer_emb, money_row)


def price_call(k, got, power, money=None):
    payload = jax.ShapeDtypeStruct((16, GT, 128), jnp.float32)
    first = k == 1
    scratch = [(8, NBUY), (LB, 128)] if first else [(4, 640), (NGOOD, 128)]
    return pl.pallas_call(
        functools.partial(price_kernel, k),
        in_specs=[VM] * (2 if first else 3),
        out_specs=[VM, VM] if first else VM,
        out_shape=[payload, jax.ShapeDtypeStruct((4, 640), jnp.float32)] if first else payload,
        scratch_shapes=[pltpu.VMEM(x, jnp.float32) for x in scratch],
        compiler_params=PARAMS,
    )(*((got, power) if first else (got, money, power)))


def utility_call(k, got, *blocks):
    if k == ITERS:
        outs, specs = [(32, 5, 128), (4, 4, 128)], [VM, VM, pl.BlockSpec(memory_space=pltpu.SMEM), VM]
    else:
        outs, specs = [(32, 4, 640), (GT, 128), (NGOOD, NBUY)], [VM] * (1 + len(blocks))
    return pl.pallas_call(
        functools.partial(utility_kernel, k),
        in_specs=specs,
        out_specs=[VM] * len(outs),
        out_shape=[jax.ShapeDtypeStruct(o, jnp.float32) for o in outs],
        scratch_shapes=[
            pltpu.VMEM((NGOOD, 128), jnp.float32),
            pltpu.VMEM((24, 128) if k == ITERS else (8, 640), jnp.float32),
        ],
        compiler_params=PARAMS,
    )(got, *blocks)


def pack_kernel(place_ref, hidden_ref, keep_ref, go_ref):
    x, zh, c = place_ref[0], place_ref[1], place_ref[2]
    rows = hidden_ref[...].astype(jnp.float32).T

    def of(to_x, to_zh, to_c):
        at = 80 * (4 * to_x + 2 * to_zh + to_c)
        return rows[at : at + 80]

    for to_x in range(4):
        for to_zh in range(2):
            plain = jnp.concatenate([of(to_x, to_zh, 0), of(to_x, to_zh, 1)], 1)
            turned = jnp.concatenate([of(to_x, to_zh, 1), of(to_x, to_zh, 0)], 1)
            part = jnp.where(c == 0, plain, turned).astype(jnp.bfloat16)
            at = (to_x + 4 - x) & 3

            @pl.when(zh == to_zh)
            def _(at=at, part=part):
                keep_ref[at] = part

            @pl.when(zh != to_zh)
            def _(at=at, part=part):
                go_ref[at] = part


def pair_kernel(mine_ref, came_ref, here_ref, across_ref):
    for d in range(4):
        mine, came = mine_ref[d].astype(jnp.float32), came_ref[d].astype(jnp.float32)
        here_ref[d] = jnp.concatenate([mine[:, 0:64], came[:, 0:64]], 1).astype(jnp.bfloat16)
        across_ref[d] = jnp.concatenate([mine[:, 64:128], came[:, 64:128]], 1).astype(jnp.bfloat16)


def buyers_kernel(place_ref, proj_ref, *refs):
    got, (out_ref, weights) = refs[:8], refs[8:]
    x, zh, c = place_ref[0], place_ref[1], place_ref[2]
    total = jnp.zeros((80, E), jnp.float32)
    for q in range(8):
        at = ((x + 4 - q // 2) & 3) * 4 + ((c + q % 2) & 1)
        weights[q, 0:64] = proj_ref[at + 2 * zh]
        weights[q, 64:128] = proj_ref[at + 2 - 2 * zh]
        total = total + jnp.dot(got[q][...], weights[q], preferred_element_type=jnp.float32)
    emb = total.astype(jnp.bfloat16)
    for p in range(out_ref.shape[0]):
        out_ref[p] = emb


def tiles_kernel(hidden_ref, out_ref):
    for t in range(16):
        top = hidden_ref[0:16, 128 * t : 128 * t + 128].astype(jnp.float32)
        low = hidden_ref[16:32, 128 * t : 128 * t + 128].astype(jnp.float32)
        out_ref[2 * t] = jnp.concatenate([top[:, 0:64], low[:, 0:64]], 1).astype(jnp.bfloat16)
        out_ref[2 * t + 1] = jnp.concatenate([top[:, 64:128], low[:, 64:128]], 1).astype(jnp.bfloat16)


def goods_kernel(got_ref, proj_ref, out_ref):
    hidden = got_ref[...].reshape(512, 128).astype(jnp.float32).T.astype(jnp.bfloat16)
    halves = [
        jnp.dot(hidden[64 * h : 64 * h + 64], proj_ref[:, h].reshape(512, E), preferred_element_type=jnp.float32)
        for h in range(2)
    ]
    emb = (halves[0] + halves[1]).astype(jnp.bfloat16)
    for p in range(out_ref.shape[0]):
        out_ref[p] = emb


def small_call(kernel, outs, *args, scratch=(), smem=0):
    return pl.pallas_call(
        kernel,
        in_specs=[pl.BlockSpec(memory_space=pltpu.SMEM)] * smem + [VM] * (len(args) - smem),
        out_specs=jax.tree.map(lambda _: VM, outs),
        out_shape=outs,
        scratch_shapes=list(scratch),
        compiler_params=PARAMS,
    )(*args)


def exchange(x, axes):
    return lax.all_to_all(x, axes, 0, 0, tiled=True)


def swap(x, axis):
    return lax.ppermute(x, axis, [(0, 1), (1, 0)])


def embeddings(buyer_hidden, goods_hidden, buyer_proj, goods_proj, place):
    bf16 = jnp.bfloat16
    shape = jax.ShapeDtypeStruct
    keep, go = small_call(pack_kernel, (shape((4, 80, 128), bf16),) * 2, place, buyer_hidden.T, smem=1)
    came = swap(go, "zh")
    here, across = small_call(pair_kernel, (shape((4, 80, 128), bf16),) * 2, keep, came)
    across = swap(across, "c")
    parts = [here[0], across[0]]
    for d in range(1, 4):
        two = jnp.stack([here[d], across[d]])
        two = lax.ppermute(two, "x", [(i, (i + d) % 4) for i in range(4)])
        parts += [two[0], two[1]]
    tiles = small_call(tiles_kernel, shape((32, 16, 128), bf16), goods_hidden.T)
    tiles = exchange(tiles, ("y", "zl"))
    goods_own = small_call(goods_kernel, shape((16, 64, E), bf16), tiles, goods_proj.reshape(32, 2, 16, E))
    goods_emb = exchange(goods_own, RING)
    buyer_own = small_call(
        buyers_kernel, shape((32, 80, E), bf16), place, buyer_proj.reshape(16, 64, E), *parts,
        scratch=(pltpu.VMEM((8, 128, E), bf16),), smem=1,
    )
    buyer_own, goods_emb = lax.optimization_barrier((buyer_own, goods_emb))
    buyer_emb = exchange(buyer_own, PLANE)
    return buyer_emb.reshape(-1, E), goods_emb.reshape(-1, E)


def per_device(buyer_hidden, goods_hidden, buyer_proj, goods_proj, endowment):
    x, y, zh, c = (lax.axis_index(a) for a in ("x", "y", "zh", "c"))
    place = jnp.stack([x, zh, c])
    buyer_emb, goods_emb = embeddings(buyer_hidden, goods_hidden, buyer_proj, goods_proj, place)

    mine = lax.dynamic_index_in_dim(endowment.reshape(4, 2, 160), zh, 1, keepdims=False).reshape(5, 128)
    money_row = lax.dynamic_slice(mine, (jnp.minimum(x * 2 + c, 4), 0), (1, 128))

    values, sent = values_call(goods_emb, buyer_emb, money_row)
    got = exchange(sent, PLANE)
    sent, money = price_call(1, got, values)
    sent, _, square = utility_call(1, exchange(sent, RING), values)
    sent = price_call(2, exchange(sent, PLANE), square, money)
    sent, before, cube = utility_call(2, exchange(sent, RING), values, square)
    got = exchange(sent, PLANE)
    sent = price_call(3, got, cube, money)
    sent, halves = utility_call(3, exchange(sent, RING), before, zh.reshape(1), square)
    final = exchange(sent, PLANE)
    own = lambda a, axis: lax.dynamic_index_in_dim(a, y, axis, keepdims=False)
    before = (own(money, 0) / jnp.sum(own(got, 1), 0)).reshape(5, 128)
    mine_total = jnp.sum(final, 0) * before
    other = swap(mine_total, "zh")
    prices = exchange(lax.optimization_barrier((halves, mine_total))[0], ("y",)).reshape(-1)
    first = jnp.where(zh == 0, mine_total, other).reshape(4, 160)
    second = jnp.where(zh == 0, other, mine_total).reshape(4, 160)
    utility = jnp.stack([first, second], 1).reshape(-1)
    return (prices, utility)


def solution(mesh):
    fine = Mesh(mesh.devices.reshape([n for _, n in FINE]), [a for a, _ in FINE])
    buyers, goods = ("y", "zl"), ("x", "zh", "c")
    placed = (P(buyers, goods), P(goods, buyers), P(), P(), P(buyers))
    return jax.shard_map(
        per_device, mesh=fine, in_specs=placed, out_specs=(P(goods), P(buyers)), check_vma=False
    )
```

```python
import functools

import jax
import jax.numpy as jnp
from jax import lax
from jax.experimental import pallas as pl
from jax.experimental.pallas import tpu as pltpu
from jax.sharding import Mesh, PartitionSpec as P

ITERS = 3
FINE = (("y", 4), ("zl", 8), ("x", 4), ("zh", 2), ("c", 2))
PLANE = ("y", "x", "c")
RING = ("zh", "zl")


E = 128
NBUY = 2560
NGOOD = 1024
LB = NBUY // 128
GT = NGOOD // 128


LOG2E = 1.4426950408889634
LN2 = 0.6931471805599453


def softplus_of(products):
    t = products * (E ** (-0.5) * LOG2E)
    u = jnp.exp2(jnp.minimum(t, 126.0))
    small = u * (LOG2E - (0.5 * LOG2E) * u)
    return jnp.maximum(t, jnp.where(u < 2.0**-8, small, jnp.log2(1.0 + u))) * LN2


def values_kernel(goods_ref, buyers_ref, money_ref, values_ref, out_ref, total, rows):
    step = pl.program_id(0)

    @pl.when(step == 0)
    def _():
        total[...] = jnp.zeros_like(total)

    for b in range(NBUY // 256):
        cols = slice(256 * b, 256 * b + 256)
        scores = lax.dot_general(
            goods_ref[...], buyers_ref[cols, :], (((1,), (1,)), ((), ())), preferred_element_type=jnp.float32
        )
        rounded = softplus_of(scores).astype(jnp.bfloat16)
        values_ref[:, cols] = rounded
        total[:, cols] += jnp.sum(rounded.astype(jnp.float32).reshape(-1, 8, 256), 0)

    @pl.when(step == pl.num_programs(0) - 1)
    def _():
        whole = jnp.sum(total[...], 0, keepdims=True)
        for b in range(LB):
            rows[b : b + 1, :] = whole[:, 128 * b : 128 * b + 128]
        rows[LB : LB + 1, :] = money_ref[...]
        for p in range(out_ref.shape[0]):
            out_ref[p] = rows[0 : LB + 1, :]


def three_parts(x, lhs):
    lhs[...] = jnp.zeros_like(lhs)
    for i in range(3):
        part = x.astype(jnp.bfloat16).astype(jnp.float32)
        x = x - part
        for b in range(part.shape[0]):
            lhs[i : i + 1, 128 * b : 128 * b + 128] = part[b : b + 1, :]


def price_kernel(k, got_ref, *refs):
    if k == 1:
        values, out_ref, money_ref, lhs, money = refs
        for b in range(LB):
            row = got_ref[8 * (b // 5) + b % 5, LB : LB + 1, :]
            money[b : b + 1, :] = row
            money_ref[b // 5 : b // 5 + 1, 128 * (b % 5) : 128 * (b % 5) + 128] = row
        total = got_ref[0, 0:LB, :]
        for p in range(1, got_ref.shape[0]):
            total = total + got_ref[p, 0:LB, :]
        three_parts(money[...] / total, lhs)
        products = lax.dot_general(
            lhs[...].astype(jnp.bfloat16), values[...], (((1,), (1,)), ((), ())), preferred_element_type=jnp.float32
        )
        whole = jnp.sum(products, 0, keepdims=True)
        rows = [whole[:, 128 * q : 128 * q + 128] for q in range(GT)]
    else:
        money_ref, power, out_ref, scale, sums = refs
        total = got_ref[0]
        for p in range(1, got_ref.shape[0]):
            total = total + got_ref[p]
        scale[...] = money_ref[...] / total

        def chunk(i, _):
            at = pl.ds(pl.multiple_of(16 * i, 16), 16)
            two = [None, None]
            for b in range(LB):
                part = scale[b // 5 : b // 5 + 1, 128 * (b % 5) : 128 * (b % 5) + 128]
                term = power[at, 128 * b : 128 * b + 128] * part
                two[b % 2] = term if two[b % 2] is None else two[b % 2] + term
            sums[at, :] = two[0] + two[1]
            return 0

        lax.fori_loop(0, NGOOD // 16, chunk, 0, unroll=4)
        rows = [jnp.sum(sums[128 * q : 128 * q + 128, :].T, 0, keepdims=True) for q in range(GT)]
    for q in range(GT):
        for p in range(out_ref.shape[0]):
            out_ref[p, q : q + 1, :] = rows[q]


def utility_kernel(k, got_ref, *refs):
    if k == 1:
        values, out_ref, sum_ref, power, inverse, rows = refs
    elif k == 2:
        values, square, out_ref, sum_ref, power, inverse, rows = refs
    else:
        before_ref, zh_ref, square, out_ref, prices_ref, inverse, rows = refs
    total = got_ref[0]
    for p in range(1, got_ref.shape[0]):
        total = total + got_ref[p]
    if k == ITERS:
        rows[0:8, :] = total / before_ref[...]
        half = rows[pl.ds(pl.multiple_of(4 * zh_ref[0], 4), 4), :]
        for p in range(prices_ref.shape[0]):
            prices_ref[p] = half
    else:
        sum_ref[...] = total
    ratio = 1.0 / total
    for q in range(GT):
        inverse[128 * q : 128 * q + 128, :] = jnp.broadcast_to(ratio[q : q + 1, :], (128, 128)).T

    def chunk(i, accs):
        at = pl.ds(pl.multiple_of(16 * i, 16), 16)
        c = inverse[at, :]
        new = []
        for b in range(LB):
            cols = slice(128 * b, 128 * b + 128)
            if k == 1:
                v = values[at, cols].astype(jnp.float32)
                raised = v * v
            elif k == 2:
                raised = square[at, cols] * values[at, cols].astype(jnp.float32)
            else:
                v = square[at, cols]
                raised = v * v
            if k < ITERS:
                power[at, cols] = raised
            term = raised * c
            new.append(accs[b] + (term[0:8] + term[8:16]))
        return tuple(new)

    accs = tuple(jnp.zeros((8, 128), jnp.float32) for _ in range(LB))
    accs = lax.fori_loop(0, NGOOD // 16, chunk, accs, unroll=2)
    for b in range(LB):
        row = jnp.sum(accs[b], 0, keepdims=True)
        if k == ITERS:
            rows[b : b + 1, :] = row
        else:
            rows[b // 5 : b // 5 + 1, 128 * (b % 5) : 128 * (b % 5) + 128] = row
    for p in range(out_ref.shape[0]):
        out_ref[p] = rows[5 * (p // 8) : 5 * (p // 8) + 5, :] if k == ITERS else rows[0:4, :]


VM = pl.BlockSpec(memory_space=pltpu.VMEM)
PARAMS = pltpu.CompilerParams(vmem_limit_bytes=16 << 20)


def values_call(goods_emb, buyer_emb, money_row):
    return pl.pallas_call(
        values_kernel,
        grid=(GT,),
        in_specs=[
            pl.BlockSpec((128, E), lambda i: (i, 0)),
            pl.BlockSpec((NBUY, E), lambda i: (0, 0)),
            pl.BlockSpec((1, 128), lambda i: (0, 0)),
        ],
        out_specs=[
            pl.BlockSpec((128, NBUY), lambda i: (i, 0)),
            pl.BlockSpec((32, LB + 1, 128), lambda i: (0, 0, 0)),
        ],
        out_shape=[
            jax.ShapeDtypeStruct((NGOOD, NBUY), jnp.bfloat16),
            jax.ShapeDtypeStruct((32, LB + 1, 128), jnp.float32),
        ],
        scratch_shapes=[pltpu.VMEM((8, NBUY), jnp.float32), pltpu.VMEM((24, 128), jnp.float32)],
        compiler_params=PARAMS,
    )(goods_emb, buyer_emb, money_row)


def price_call(k, got, power, money=None):
    payload = jax.ShapeDtypeStruct((16, GT, 128), jnp.float32)
    first = k == 1
    scratch = [(8, NBUY), (LB, 128)] if first else [(4, 640), (NGOOD, 128)]
    return pl.pallas_call(
        functools.partial(price_kernel, k),
        in_specs=[VM] * (2 if first else 3),
        out_specs=[VM, VM] if first else VM,
        out_shape=[payload, jax.ShapeDtypeStruct((4, 640), jnp.float32)] if first else payload,
        scratch_shapes=[pltpu.VMEM(x, jnp.float32) for x in scratch],
        compiler_params=PARAMS,
    )(*((got, power) if first else (got, money, power)))


def utility_call(k, got, *blocks):
    if k == ITERS:
        outs, specs = [(32, 5, 128), (4, 4, 128)], [VM, VM, pl.BlockSpec(memory_space=pltpu.SMEM), VM]
    else:
        outs, specs = [(32, 4, 640), (GT, 128), (NGOOD, NBUY)], [VM] * (1 + len(blocks))
    return pl.pallas_call(
        functools.partial(utility_kernel, k),
        in_specs=specs,
        out_specs=[VM] * len(outs),
        out_shape=[jax.ShapeDtypeStruct(o, jnp.float32) for o in outs],
        scratch_shapes=[
            pltpu.VMEM((NGOOD, 128), jnp.float32),
            pltpu.VMEM((24, 128) if k == ITERS else (8, 640), jnp.float32),
        ],
        compiler_params=PARAMS,
    )(got, *blocks)


def pack_kernel(place_ref, hidden_ref, goods_ref, keep_ref, go_ref, tiles_ref):
    x, zh, c = place_ref[0], place_ref[1], place_ref[2]
    rows = hidden_ref[...].astype(jnp.float32).T

    def of(to_x, to_zh, to_c):
        at = 80 * (4 * to_x + 2 * to_zh + to_c)
        return rows[at : at + 80]

    for to_x in range(4):
        for to_zh in range(2):
            plain = jnp.concatenate([of(to_x, to_zh, 0), of(to_x, to_zh, 1)], 1)
            turned = jnp.concatenate([of(to_x, to_zh, 1), of(to_x, to_zh, 0)], 1)
            part = jnp.where(c == 0, plain, turned).astype(jnp.bfloat16)
            at = (to_x + 4 - x) & 3

            @pl.when(zh == to_zh)
            def _(at=at, part=part):
                keep_ref[at] = part

            @pl.when(zh != to_zh)
            def _(at=at, part=part):
                go_ref[at] = part

    for t in range(16):
        top = goods_ref[0:16, 128 * t : 128 * t + 128].astype(jnp.float32)
        low = goods_ref[16:32, 128 * t : 128 * t + 128].astype(jnp.float32)
        tiles_ref[2 * t] = jnp.concatenate([top[:, 0:64], low[:, 0:64]], 1).astype(jnp.bfloat16)
        tiles_ref[2 * t + 1] = jnp.concatenate([top[:, 64:128], low[:, 64:128]], 1).astype(jnp.bfloat16)


def pair_kernel(mine_ref, came_ref, here_ref, across_ref):
    for d in range(4):
        mine, came = mine_ref[d].astype(jnp.float32), came_ref[d].astype(jnp.float32)
        here_ref[d] = jnp.concatenate([mine[:, 0:64], came[:, 0:64]], 1).astype(jnp.bfloat16)
        across_ref[d] = jnp.concatenate([mine[:, 64:128], came[:, 64:128]], 1).astype(jnp.bfloat16)


def buyers_kernel(place_ref, proj_ref, *refs):
    got, out_ref = refs[:8], refs[8]
    x, c = place_ref[0], place_ref[2]
    total = jnp.zeros((80, E), jnp.float32)
    for q in range(8):
        at = ((x + 4 - q // 2) & 3) * 2 + ((c + q % 2) & 1)
        total = total + jnp.dot(got[q][...], proj_ref[at], preferred_element_type=jnp.float32)
    emb = total.astype(jnp.bfloat16)
    for p in range(out_ref.shape[0]):
        out_ref[p] = emb


def goods_kernel(got_ref, proj_ref, out_ref):
    hidden = got_ref[...].reshape(512, 128).astype(jnp.float32).T.astype(jnp.bfloat16)
    halves = [
        jnp.dot(hidden[64 * h : 64 * h + 64], proj_ref[h].reshape(512, E), preferred_element_type=jnp.float32)
        for h in range(2)
    ]
    emb = (halves[0] + halves[1]).astype(jnp.bfloat16)
    for p in range(out_ref.shape[0]):
        out_ref[p] = emb


def small_call(kernel, outs, *args, scratch=(), smem=0):
    return pl.pallas_call(
        kernel,
        in_specs=[pl.BlockSpec(memory_space=pltpu.SMEM)] * smem + [VM] * (len(args) - smem),
        out_specs=jax.tree.map(lambda _: VM, outs),
        out_shape=outs,
        scratch_shapes=list(scratch),
        compiler_params=PARAMS,
    )(*args)


def exchange(x, axes):
    return lax.all_to_all(x, axes, 0, 0, tiled=True)


def swap(x, axis):
    return lax.ppermute(x, axis, [(0, 1), (1, 0)])


def embeddings(buyer_hidden, goods_hidden, buyer_proj, goods_proj, place):
    bf16 = jnp.bfloat16
    shape = jax.ShapeDtypeStruct
    outs = (shape((4, 80, 128), bf16), shape((4, 80, 128), bf16), shape((32, 16, 128), bf16))
    keep, go, tiles = small_call(pack_kernel, outs, place, buyer_hidden.T, goods_hidden.T, smem=1)
    came = swap(go, "zh")
    here, across = small_call(pair_kernel, (shape((4, 80, 128), bf16),) * 2, keep, came)
    across = swap(across, "c")
    parts = [here[0], across[0]]
    for d in range(1, 4):
        two = jnp.stack([here[d], across[d]])
        two = lax.ppermute(two, "x", [(i, (i + d) % 4) for i in range(4)])
        parts += [two[0], two[1]]
    tiles = exchange(tiles, ("y", "zl"))
    goods_own = small_call(goods_kernel, shape((16, 64, E), bf16), tiles, goods_proj.reshape(32, 2, 16, E).transpose(1, 0, 2, 3))
    goods_emb = exchange(goods_own, RING)
    proj = buyer_proj.reshape(4, 2, 2, 64, E)
    proj = jnp.where(place[1] == 0, proj, proj[:, ::-1]).transpose(0, 2, 1, 3, 4).reshape(8, 128, E)
    buyer_own = small_call(buyers_kernel, shape((32, 80, E), bf16), place, proj, *parts, smem=1)
    buyer_own, goods_emb = lax.optimization_barrier((buyer_own, goods_emb))
    buyer_emb = exchange(buyer_own, PLANE)
    return buyer_emb.reshape(-1, E), goods_emb.reshape(-1, E)


def per_device(buyer_hidden, goods_hidden, buyer_proj, goods_proj, endowment):
    x, y, zh, c = (lax.axis_index(a) for a in ("x", "y", "zh", "c"))
    place = jnp.stack([x, zh, c])
    buyer_emb, goods_emb = embeddings(buyer_hidden, goods_hidden, buyer_proj, goods_proj, place)

    mine = lax.dynamic_index_in_dim(endowment.reshape(4, 2, 160), zh, 1, keepdims=False).reshape(5, 128)
    money_row = lax.dynamic_slice(mine, (jnp.minimum(x * 2 + c, 4), 0), (1, 128))

    values, sent = values_call(goods_emb, buyer_emb, money_row)
    got = exchange(sent, PLANE)
    sent, money = price_call(1, got, values)
    sent, _, square = utility_call(1, exchange(sent, RING), values)
    sent = price_call(2, exchange(sent, PLANE), square, money)
    sent, before, cube = utility_call(2, exchange(sent, RING), values, square)
    got = exchange(sent, PLANE)
    sent = price_call(3, got, cube, money)
    sent, halves = utility_call(3, exchange(sent, RING), before, zh.reshape(1), square)
    final = exchange(sent, PLANE)
    own = lambda a, axis: lax.dynamic_index_in_dim(a, y, axis, keepdims=False)
    before = (own(money, 0) / jnp.sum(own(got, 1), 0)).reshape(5, 128)
    mine_total = jnp.sum(final, 0) * before
    other = swap(mine_total, "zh")
    prices = exchange(lax.optimization_barrier((halves, mine_total))[0], ("y",)).reshape(-1)
    first = jnp.where(zh == 0, mine_total, other).reshape(4, 160)
    second = jnp.where(zh == 0, other, mine_total).reshape(4, 160)
    utility = jnp.stack([first, second], 1).reshape(-1)
    return (prices, utility)


def solution(mesh):
    fine = Mesh(mesh.devices.reshape([n for _, n in FINE]), [a for a, _ in FINE])
    buyers, goods = ("y", "zl"), ("x", "zh", "c")
    placed = (P(buyers, goods), P(goods, buyers), P(), P(), P(buyers))
    return jax.shard_map(
        per_device, mesh=fine, in_specs=placed, out_specs=(P(goods), P(buyers)), check_vma=False
    )
```

```python
import functools

import jax
import jax.numpy as jnp
from jax import lax
from jax.experimental import pallas as pl
from jax.experimental.pallas import tpu as pltpu
from jax.sharding import Mesh, PartitionSpec as P

ITERS = 3
FINE = (("y", 4), ("zl", 8), ("x", 4), ("zh", 2), ("c", 2))
PLANE = ("y", "x", "c")
RING = ("zh", "zl")


E = 128
NBUY = 2560
NGOOD = 1024
LB = NBUY // 128
GT = NGOOD // 128


LOG2E = 1.4426950408889634
LN2 = 0.6931471805599453


def softplus_of(products):
    t = products * (E ** (-0.5) * LOG2E)
    u = jnp.exp2(jnp.minimum(t, 126.0))
    small = u * (LOG2E - (0.5 * LOG2E) * u)
    return jnp.maximum(t, jnp.where(u < 2.0**-8, small, jnp.log2(1.0 + u))) * LN2


def values_kernel(goods_ref, buyers_ref, money_ref, values_ref, out_ref, total, rows):
    step = pl.program_id(0)

    @pl.when(step == 0)
    def _():
        total[...] = jnp.zeros_like(total)

    for b in range(NBUY // 256):
        cols = slice(256 * b, 256 * b + 256)
        scores = lax.dot_general(
            goods_ref[...], buyers_ref[cols, :], (((1,), (1,)), ((), ())), preferred_element_type=jnp.float32
        )
        rounded = softplus_of(scores).astype(jnp.bfloat16)
        values_ref[:, cols] = rounded
        total[:, cols] += jnp.sum(rounded.astype(jnp.float32).reshape(-1, 8, 256), 0)

    @pl.when(step == pl.num_programs(0) - 1)
    def _():
        whole = jnp.sum(total[...], 0, keepdims=True)
        for b in range(LB):
            rows[b : b + 1, :] = whole[:, 128 * b : 128 * b + 128]
        rows[LB : LB + 1, :] = money_ref[...]
        for p in range(out_ref.shape[0]):
            out_ref[p] = rows[0 : LB + 1, :]


def three_parts(x, lhs):
    lhs[...] = jnp.zeros_like(lhs)
    for i in range(3):
        part = x.astype(jnp.bfloat16).astype(jnp.float32)
        x = x - part
        for b in range(part.shape[0]):
            lhs[i : i + 1, 128 * b : 128 * b + 128] = part[b : b + 1, :]


def price_kernel(k, got_ref, *refs):
    if k == 1:
        values, out_ref, money_ref, lhs, money = refs
        for b in range(LB):
            row = got_ref[8 * (b // 5) + b % 5, LB : LB + 1, :]
            money[b : b + 1, :] = row
            money_ref[b // 5 : b // 5 + 1, 128 * (b % 5) : 128 * (b % 5) + 128] = row
        total = got_ref[0, 0:LB, :]
        for p in range(1, got_ref.shape[0]):
            total = total + got_ref[p, 0:LB, :]
        three_parts(money[...] / total, lhs)
        products = lax.dot_general(
            lhs[...].astype(jnp.bfloat16), values[...], (((1,), (1,)), ((), ())), preferred_element_type=jnp.float32
        )
        whole = jnp.sum(products, 0, keepdims=True)
        rows = [whole[:, 128 * q : 128 * q + 128] for q in range(GT)]
    else:
        money_ref, power, out_ref, scale, sums = refs
        total = got_ref[0]
        for p in range(1, got_ref.shape[0]):
            total = total + got_ref[p]
        scale[...] = money_ref[...] / total

        def chunk(i, _):
            at = pl.ds(pl.multiple_of(16 * i, 16), 16)
            two = [None, None]
            for b in range(LB):
                part = scale[b // 5 : b // 5 + 1, 128 * (b % 5) : 128 * (b % 5) + 128]
                term = power[at, 128 * b : 128 * b + 128] * part
                two[b % 2] = term if two[b % 2] is None else two[b % 2] + term
            sums[at, :] = two[0] + two[1]
            return 0

        lax.fori_loop(0, NGOOD // 16, chunk, 0, unroll=4)
        rows = [jnp.sum(sums[128 * q : 128 * q + 128, :].T, 0, keepdims=True) for q in range(GT)]
    for q in range(GT):
        for p in range(out_ref.shape[0]):
            out_ref[p, q : q + 1, :] = rows[q]


def utility_kernel(k, got_ref, *refs):
    if k == 1:
        values, out_ref, sum_ref, power, inverse, rows = refs
    elif k == 2:
        values, square, out_ref, sum_ref, power, inverse, rows = refs
    else:
        before_ref, zh_ref, square, out_ref, prices_ref, inverse, rows = refs
    total = got_ref[0]
    for p in range(1, got_ref.shape[0]):
        total = total + got_ref[p]
    if k == ITERS:
        rows[0:8, :] = total / before_ref[...]
        half = rows[pl.ds(pl.multiple_of(4 * zh_ref[0], 4), 4), :]
        for p in range(prices_ref.shape[0]):
            prices_ref[p] = half
    else:
        sum_ref[...] = total
    ratio = 1.0 / total
    for q in range(GT):
        inverse[128 * q : 128 * q + 128, :] = jnp.broadcast_to(ratio[q : q + 1, :], (128, 128)).T

    def chunk(i, accs):
        at = pl.ds(pl.multiple_of(16 * i, 16), 16)
        c = inverse[at, :]
        new = []
        for b in range(LB):
            cols = slice(128 * b, 128 * b + 128)
            if k == 1:
                v = values[at, cols].astype(jnp.float32)
                raised = v * v
            elif k == 2:
                raised = square[at, cols] * values[at, cols].astype(jnp.float32)
            else:
                v = square[at, cols]
                raised = v * v
            if k < ITERS:
                power[at, cols] = raised
            term = raised * c
            new.append(accs[b] + (term[0:8] + term[8:16]))
        return tuple(new)

    accs = tuple(jnp.zeros((8, 128), jnp.float32) for _ in range(LB))
    accs = lax.fori_loop(0, NGOOD // 16, chunk, accs, unroll=2)
    for b in range(LB):
        row = jnp.sum(accs[b], 0, keepdims=True)
        if k == ITERS:
            rows[b : b + 1, :] = row
        else:
            rows[b // 5 : b // 5 + 1, 128 * (b % 5) : 128 * (b % 5) + 128] = row
    for p in range(out_ref.shape[0]):
        out_ref[p] = rows[5 * (p // 8) : 5 * (p // 8) + 5, :] if k == ITERS else rows[0:4, :]


VM = pl.BlockSpec(memory_space=pltpu.VMEM)
PARAMS = pltpu.CompilerParams(vmem_limit_bytes=16 << 20)


def values_call(goods_emb, buyer_emb, money_row):
    return pl.pallas_call(
        values_kernel,
        grid=(NGOOD // 256,),
        in_specs=[
            pl.BlockSpec((256, E), lambda i: (i, 0)),
            pl.BlockSpec((NBUY, E), lambda i: (0, 0)),
            pl.BlockSpec((1, 128), lambda i: (0, 0)),
        ],
        out_specs=[
            pl.BlockSpec((256, NBUY), lambda i: (i, 0)),
            pl.BlockSpec((32, LB + 1, 128), lambda i: (0, 0, 0)),
        ],
        out_shape=[
            jax.ShapeDtypeStruct((NGOOD, NBUY), jnp.bfloat16),
            jax.ShapeDtypeStruct((32, LB + 1, 128), jnp.float32),
        ],
        scratch_shapes=[pltpu.VMEM((8, NBUY), jnp.float32), pltpu.VMEM((24, 128), jnp.float32)],
        compiler_params=PARAMS,
    )(goods_emb, buyer_emb, money_row)


def price_call(k, got, power, money=None):
    payload = jax.ShapeDtypeStruct((16, GT, 128), jnp.float32)
    first = k == 1
    scratch = [(8, NBUY), (LB, 128)] if first else [(4, 640), (NGOOD, 128)]
    return pl.pallas_call(
        functools.partial(price_kernel, k),
        in_specs=[VM] * (2 if first else 3),
        out_specs=[VM, VM] if first else VM,
        out_shape=[payload, jax.ShapeDtypeStruct((4, 640), jnp.float32)] if first else payload,
        scratch_shapes=[pltpu.VMEM(x, jnp.float32) for x in scratch],
        compiler_params=PARAMS,
    )(*((got, power) if first else (got, money, power)))


def utility_call(k, got, *blocks):
    if k == ITERS:
        outs, specs = [(32, 5, 128), (4, 4, 128)], [VM, VM, pl.BlockSpec(memory_space=pltpu.SMEM), VM]
    else:
        outs, specs = [(32, 4, 640), (GT, 128), (NGOOD, NBUY)], [VM] * (1 + len(blocks))
    return pl.pallas_call(
        functools.partial(utility_kernel, k),
        in_specs=specs,
        out_specs=[VM] * len(outs),
        out_shape=[jax.ShapeDtypeStruct(o, jnp.float32) for o in outs],
        scratch_shapes=[
            pltpu.VMEM((NGOOD, 128), jnp.float32),
            pltpu.VMEM((24, 128) if k == ITERS else (8, 640), jnp.float32),
        ],
        compiler_params=PARAMS,
    )(got, *blocks)


def pack_kernel(place_ref, hidden_ref, goods_ref, keep_ref, go_ref, tiles_ref):
    x, zh, c = place_ref[0], place_ref[1], place_ref[2]
    rows = hidden_ref[...].astype(jnp.float32).T

    def of(to_x, to_zh, to_c):
        at = 80 * (4 * to_x + 2 * to_zh + to_c)
        return rows[at : at + 80]

    for to_x in range(4):
        for to_zh in range(2):
            plain = jnp.concatenate([of(to_x, to_zh, 0), of(to_x, to_zh, 1)], 1)
            turned = jnp.concatenate([of(to_x, to_zh, 1), of(to_x, to_zh, 0)], 1)
            part = jnp.where(c == 0, plain, turned).astype(jnp.bfloat16)
            at = (to_x + 4 - x) & 3

            @pl.when(zh == to_zh)
            def _(at=at, part=part):
                keep_ref[at] = part

            @pl.when(zh != to_zh)
            def _(at=at, part=part):
                go_ref[at] = part

    for t in range(16):
        top = goods_ref[0:16, 128 * t : 128 * t + 128].astype(jnp.float32)
        low = goods_ref[16:32, 128 * t : 128 * t + 128].astype(jnp.float32)
        tiles_ref[2 * t] = jnp.concatenate([top[:, 0:64], low[:, 0:64]], 1).astype(jnp.bfloat16)
        tiles_ref[2 * t + 1] = jnp.concatenate([top[:, 64:128], low[:, 64:128]], 1).astype(jnp.bfloat16)


def pair_kernel(mine_ref, came_ref, here_ref, across_ref):
    for d in range(4):
        mine, came = mine_ref[d].astype(jnp.float32), came_ref[d].astype(jnp.float32)
        here_ref[d] = jnp.concatenate([mine[:, 0:64], came[:, 0:64]], 1).astype(jnp.bfloat16)
        across_ref[d] = jnp.concatenate([mine[:, 64:128], came[:, 64:128]], 1).astype(jnp.bfloat16)


def buyers_kernel(place_ref, proj_ref, *refs):
    got, out_ref = refs[:8], refs[8]
    x, c = place_ref[0], place_ref[2]
    total = jnp.zeros((80, E), jnp.float32)
    for q in range(8):
        at = ((x + 4 - q // 2) & 3) * 2 + ((c + q % 2) & 1)
        total = total + jnp.dot(got[q][...], proj_ref[at], preferred_element_type=jnp.float32)
    emb = total.astype(jnp.bfloat16)
    for p in range(out_ref.shape[0]):
        out_ref[p] = emb


def goods_kernel(got_ref, proj_ref, out_ref):
    hidden = got_ref[...].reshape(512, 128).astype(jnp.float32).T.astype(jnp.bfloat16)
    halves = [
        jnp.dot(hidden[64 * h : 64 * h + 64], proj_ref[h].reshape(512, E), preferred_element_type=jnp.float32)
        for h in range(2)
    ]
    emb = (halves[0] + halves[1]).astype(jnp.bfloat16)
    for p in range(out_ref.shape[0]):
        out_ref[p] = emb


def small_call(kernel, outs, *args, scratch=(), smem=0):
    return pl.pallas_call(
        kernel,
        in_specs=[pl.BlockSpec(memory_space=pltpu.SMEM)] * smem + [VM] * (len(args) - smem),
        out_specs=jax.tree.map(lambda _: VM, outs),
        out_shape=outs,
        scratch_shapes=list(scratch),
        compiler_params=PARAMS,
    )(*args)


def exchange(x, axes):
    return lax.all_to_all(x, axes, 0, 0, tiled=True)


def swap(x, axis):
    return lax.ppermute(x, axis, [(0, 1), (1, 0)])


def embeddings(buyer_hidden, goods_hidden, buyer_proj, goods_proj, place):
    bf16 = jnp.bfloat16
    shape = jax.ShapeDtypeStruct
    outs = (shape((4, 80, 128), bf16), shape((4, 80, 128), bf16), shape((32, 16, 128), bf16))
    keep, go, tiles = small_call(pack_kernel, outs, place, buyer_hidden.T, goods_hidden.T, smem=1)
    came = swap(go, "zh")
    here, across = small_call(pair_kernel, (shape((4, 80, 128), bf16),) * 2, keep, came)
    across = swap(across, "c")
    parts = [here[0], across[0]]
    for d in range(1, 4):
        two = jnp.stack([here[d], across[d]])
        two = lax.ppermute(two, "x", [(i, (i + d) % 4) for i in range(4)])
        parts += [two[0], two[1]]
    tiles = exchange(tiles, ("y", "zl"))
    goods_own = small_call(goods_kernel, shape((16, 64, E), bf16), tiles, goods_proj.reshape(32, 2, 16, E).transpose(1, 0, 2, 3))
    goods_emb = exchange(goods_own, RING)
    proj = buyer_proj.reshape(4, 2, 2, 64, E)
    proj = jnp.where(place[1] == 0, proj, proj[:, ::-1]).transpose(0, 2, 1, 3, 4).reshape(8, 128, E)
    buyer_own = small_call(buyers_kernel, shape((32, 80, E), bf16), place, proj, *parts, smem=1)
    buyer_own, goods_emb = lax.optimization_barrier((buyer_own, goods_emb))
    buyer_emb = exchange(buyer_own, PLANE)
    return buyer_emb.reshape(-1, E), goods_emb.reshape(-1, E)


def per_device(buyer_hidden, goods_hidden, buyer_proj, goods_proj, endowment):
    x, y, zh, c = (lax.axis_index(a) for a in ("x", "y", "zh", "c"))
    place = jnp.stack([x, zh, c])
    buyer_emb, goods_emb = embeddings(buyer_hidden, goods_hidden, buyer_proj, goods_proj, place)

    mine = lax.dynamic_index_in_dim(endowment.reshape(4, 2, 160), zh, 1, keepdims=False).reshape(5, 128)
    money_row = lax.dynamic_slice(mine, (jnp.minimum(x * 2 + c, 4), 0), (1, 128))

    values, sent = values_call(goods_emb, buyer_emb, money_row)
    got = exchange(sent, PLANE)
    sent, money = price_call(1, got, values)
    sent, _, square = utility_call(1, exchange(sent, RING), values)
    sent = price_call(2, exchange(sent, PLANE), square, money)
    sent, before, cube = utility_call(2, exchange(sent, RING), values, square)
    got = exchange(sent, PLANE)
    sent = price_call(3, got, cube, money)
    sent, halves = utility_call(3, exchange(sent, RING), before, zh.reshape(1), square)
    final = exchange(sent, PLANE)
    own = lambda a, axis: lax.dynamic_index_in_dim(a, y, axis, keepdims=False)
    before = (own(money, 0) / jnp.sum(own(got, 1), 0)).reshape(5, 128)
    mine_total = jnp.sum(final, 0) * before
    other = swap(mine_total, "zh")
    prices = exchange(lax.optimization_barrier((halves, mine_total))[0], ("y",)).reshape(-1)
    first = jnp.where(zh == 0, mine_total, other).reshape(4, 160)
    second = jnp.where(zh == 0, other, mine_total).reshape(4, 160)
    utility = jnp.stack([first, second], 1).reshape(-1)
    return (prices, utility)


def solution(mesh):
    fine = Mesh(mesh.devices.reshape([n for _, n in FINE]), [a for a, _ in FINE])
    buyers, goods = ("y", "zl"), ("x", "zh", "c")
    placed = (P(buyers, goods), P(goods, buyers), P(), P(), P(buyers))
    return jax.shard_map(
        per_device, mesh=fine, in_specs=placed, out_specs=(P(goods), P(buyers)), check_vma=False
    )
```

```python
import functools

import jax
import jax.numpy as jnp
from jax import lax
from jax.experimental import pallas as pl
from jax.experimental.pallas import tpu as pltpu
from jax.sharding import Mesh, PartitionSpec as P

ITERS = 3
FINE = (("y", 4), ("zl", 8), ("x", 4), ("zh", 2), ("c", 2))
PLANE = ("y", "x", "c")
RING = ("zh", "zl")


E = 128
NBUY = 2560
NGOOD = 1024
LB = NBUY // 128
GT = NGOOD // 128


LOG2E = 1.4426950408889634
LN2 = 0.6931471805599453


def softplus_of(products):
    t = products * (E ** (-0.5) * LOG2E)
    u = jnp.exp2(jnp.minimum(t, 126.0))
    small = u * (LOG2E - (0.5 * LOG2E) * u)
    return jnp.maximum(t, jnp.where(u < 2.0**-8, small, jnp.log2(1.0 + u))) * LN2


def values_kernel(goods_ref, buyers_ref, money_ref, values_ref, out_ref, total, rows):
    step = pl.program_id(0)

    @pl.when(step == 0)
    def _():
        total[...] = jnp.zeros_like(total)

    for b in range(NBUY // 256):
        cols = slice(256 * b, 256 * b + 256)
        scores = lax.dot_general(
            goods_ref[...], buyers_ref[cols, :], (((1,), (1,)), ((), ())), preferred_element_type=jnp.float32
        )
        rounded = softplus_of(scores).astype(jnp.bfloat16)
        values_ref[:, cols] = rounded
        total[:, cols] += jnp.sum(rounded.astype(jnp.float32).reshape(-1, 8, 256), 0)

    @pl.when(step == pl.num_programs(0) - 1)
    def _():
        whole = jnp.sum(total[...], 0, keepdims=True)
        for b in range(LB):
            rows[b : b + 1, :] = whole[:, 128 * b : 128 * b + 128]
        rows[LB : LB + 1, :] = money_ref[...]
        for p in range(out_ref.shape[0]):
            out_ref[p] = rows[0 : LB + 1, :]


def three_parts(x, lhs):
    lhs[...] = jnp.zeros_like(lhs)
    for i in range(3):
        part = x.astype(jnp.bfloat16).astype(jnp.float32)
        x = x - part
        for b in range(part.shape[0]):
            lhs[i : i + 1, 128 * b : 128 * b + 128] = part[b : b + 1, :]


def price_kernel(k, got_ref, *refs):
    if k == 1:
        values, out_ref, money_ref, lhs, money = refs
        for b in range(LB):
            row = got_ref[8 * (b // 5) + b % 5, LB : LB + 1, :]
            money[b : b + 1, :] = row
            money_ref[b // 5 : b // 5 + 1, 128 * (b % 5) : 128 * (b % 5) + 128] = row
        total = got_ref[0, 0:LB, :]
        for p in range(1, got_ref.shape[0]):
            total = total + got_ref[p, 0:LB, :]
        three_parts(money[...] / total, lhs)
        products = lax.dot_general(
            lhs[...].astype(jnp.bfloat16), values[...], (((1,), (1,)), ((), ())), preferred_element_type=jnp.float32
        )
        whole = jnp.sum(products, 0, keepdims=True)
        rows = [whole[:, 128 * q : 128 * q + 128] for q in range(GT)]
    else:
        money_ref, power, out_ref, scale, sums = refs
        total = got_ref[0]
        for p in range(1, got_ref.shape[0]):
            total = total + got_ref[p]
        scale[...] = money_ref[...] / total

        def chunk(i, _):
            at = pl.ds(pl.multiple_of(16 * i, 16), 16)
            two = [None, None]
            for b in range(LB):
                part = scale[b // 5 : b // 5 + 1, 128 * (b % 5) : 128 * (b % 5) + 128]
                term = power[at, 128 * b : 128 * b + 128] * part
                two[b % 2] = term if two[b % 2] is None else two[b % 2] + term
            sums[at, :] = two[0] + two[1]
            return 0

        lax.fori_loop(0, NGOOD // 16, chunk, 0, unroll=4)
        rows = [jnp.sum(sums[128 * q : 128 * q + 128, :].T, 0, keepdims=True) for q in range(GT)]
    for q in range(GT):
        for p in range(out_ref.shape[0]):
            out_ref[p, q : q + 1, :] = rows[q]


def utility_kernel(k, got_ref, *refs):
    if k == 1:
        values, out_ref, sum_ref, power, inverse, rows = refs
    elif k == 2:
        values, square, out_ref, sum_ref, power, inverse, rows = refs
    else:
        before_ref, zh_ref, square, out_ref, prices_ref, inverse, rows = refs
    total = got_ref[0]
    for p in range(1, got_ref.shape[0]):
        total = total + got_ref[p]
    if k == ITERS:
        rows[0:8, :] = total / before_ref[...]
        half = rows[pl.ds(pl.multiple_of(4 * zh_ref[0], 4), 4), :]
        for p in range(prices_ref.shape[0]):
            prices_ref[p] = half
    else:
        sum_ref[...] = total
    ratio = 1.0 / total
    for q in range(GT):
        inverse[128 * q : 128 * q + 128, :] = jnp.broadcast_to(ratio[q : q + 1, :], (128, 128)).T

    def chunk(i, accs):
        at = pl.ds(pl.multiple_of(16 * i, 16), 16)
        c = inverse[at, :]
        new = []
        for b in range(LB):
            cols = slice(128 * b, 128 * b + 128)
            if k == 1:
                v = values[at, cols].astype(jnp.float32)
                raised = v * v
            elif k == 2:
                raised = square[at, cols] * values[at, cols].astype(jnp.float32)
            else:
                v = square[at, cols]
                raised = v * v
            if k < ITERS:
                power[at, cols] = raised
            term = raised * c
            new.append(accs[b] + (term[0:8] + term[8:16]))
        return tuple(new)

    accs = tuple(jnp.zeros((8, 128), jnp.float32) for _ in range(LB))
    accs = lax.fori_loop(0, NGOOD // 16, chunk, accs, unroll=2)
    for b in range(LB):
        row = jnp.sum(accs[b], 0, keepdims=True)
        if k == ITERS:
            rows[b : b + 1, :] = row
        else:
            rows[b // 5 : b // 5 + 1, 128 * (b % 5) : 128 * (b % 5) + 128] = row
    for p in range(out_ref.shape[0]):
        out_ref[p] = rows[5 * (p // 8) : 5 * (p // 8) + 5, :] if k == ITERS else rows[0:4, :]


VM = pl.BlockSpec(memory_space=pltpu.VMEM)
PARAMS = pltpu.CompilerParams(vmem_limit_bytes=16 << 20)


def values_call(goods_emb, buyer_emb, money_row):
    return pl.pallas_call(
        values_kernel,
        grid=(NGOOD // 256,),
        in_specs=[
            pl.BlockSpec((256, E), lambda i: (i, 0)),
            pl.BlockSpec((NBUY, E), lambda i: (0, 0)),
            pl.BlockSpec((1, 128), lambda i: (0, 0)),
        ],
        out_specs=[
            pl.BlockSpec((256, NBUY), lambda i: (i, 0)),
            pl.BlockSpec((32, LB + 1, 128), lambda i: (0, 0, 0)),
        ],
        out_shape=[
            jax.ShapeDtypeStruct((NGOOD, NBUY), jnp.bfloat16),
            jax.ShapeDtypeStruct((32, LB + 1, 128), jnp.float32),
        ],
        scratch_shapes=[pltpu.VMEM((8, NBUY), jnp.float32), pltpu.VMEM((24, 128), jnp.float32)],
        compiler_params=PARAMS,
    )(goods_emb, buyer_emb, money_row)


def price_call(k, got, power, money=None):
    payload = jax.ShapeDtypeStruct((16, GT, 128), jnp.float32)
    first = k == 1
    scratch = [(8, NBUY), (LB, 128)] if first else [(4, 640), (NGOOD, 128)]
    return pl.pallas_call(
        functools.partial(price_kernel, k),
        in_specs=[VM] * (2 if first else 3),
        out_specs=[VM, VM] if first else VM,
        out_shape=[payload, jax.ShapeDtypeStruct((4, 640), jnp.float32)] if first else payload,
        scratch_shapes=[pltpu.VMEM(x, jnp.float32) for x in scratch],
        compiler_params=PARAMS,
    )(*((got, power) if first else (got, money, power)))


def utility_call(k, got, *blocks):
    if k == ITERS:
        outs, specs = [(32, 5, 128), (4, 4, 128)], [VM, VM, pl.BlockSpec(memory_space=pltpu.SMEM), VM]
    else:
        outs, specs = [(32, 4, 640), (GT, 128), (NGOOD, NBUY)], [VM] * (1 + len(blocks))
    return pl.pallas_call(
        functools.partial(utility_kernel, k),
        in_specs=specs,
        out_specs=[VM] * len(outs),
        out_shape=[jax.ShapeDtypeStruct(o, jnp.float32) for o in outs],
        scratch_shapes=[
            pltpu.VMEM((NGOOD, 128), jnp.float32),
            pltpu.VMEM((24, 128) if k == ITERS else (8, 640), jnp.float32),
        ],
        compiler_params=PARAMS,
    )(got, *blocks)


def pack_kernel(place_ref, hidden_ref, goods_hbm, keep_ref, go_ref, tiles_ref, goods_ref, sem):
    copy = pltpu.make_async_copy(goods_hbm, goods_ref, sem)
    copy.start()
    x, zh, c = place_ref[0], place_ref[1], place_ref[2]
    rows = hidden_ref[...].astype(jnp.float32).T

    def of(to_x, to_zh, to_c):
        at = 80 * (4 * to_x + 2 * to_zh + to_c)
        return rows[at : at + 80]

    for to_x in range(4):
        for to_zh in range(2):
            plain = jnp.concatenate([of(to_x, to_zh, 0), of(to_x, to_zh, 1)], 1)
            turned = jnp.concatenate([of(to_x, to_zh, 1), of(to_x, to_zh, 0)], 1)
            part = jnp.where(c == 0, plain, turned).astype(jnp.bfloat16)
            at = (to_x + 4 - x) & 3

            @pl.when(zh == to_zh)
            def _(at=at, part=part):
                keep_ref[at] = part

            @pl.when(zh != to_zh)
            def _(at=at, part=part):
                go_ref[at] = part

    copy.wait()
    for t in range(16):
        top = goods_ref[0:16, 128 * t : 128 * t + 128].astype(jnp.float32)
        low = goods_ref[16:32, 128 * t : 128 * t + 128].astype(jnp.float32)
        tiles_ref[2 * t] = jnp.concatenate([top[:, 0:64], low[:, 0:64]], 1).astype(jnp.bfloat16)
        tiles_ref[2 * t + 1] = jnp.concatenate([top[:, 64:128], low[:, 64:128]], 1).astype(jnp.bfloat16)


def pair_kernel(mine_ref, came_ref, here_ref, across_ref):
    for d in range(4):
        mine, came = mine_ref[d].astype(jnp.float32), came_ref[d].astype(jnp.float32)
        here_ref[d] = jnp.concatenate([mine[:, 0:64], came[:, 0:64]], 1).astype(jnp.bfloat16)
        across_ref[d] = jnp.concatenate([mine[:, 64:128], came[:, 64:128]], 1).astype(jnp.bfloat16)


def buyers_kernel(place_ref, proj_ref, *refs):
    got, out_ref = refs[:8], refs[8]
    x, c = place_ref[0], place_ref[2]
    total = jnp.zeros((80, E), jnp.float32)
    for q in range(8):
        at = ((x + 4 - q // 2) & 3) * 2 + ((c + q % 2) & 1)
        total = total + jnp.dot(got[q][...], proj_ref[at], preferred_element_type=jnp.float32)
    emb = total.astype(jnp.bfloat16)
    for p in range(out_ref.shape[0]):
        out_ref[p] = emb


def goods_kernel(got_ref, proj_ref, out_ref):
    hidden = got_ref[...].reshape(512, 128).astype(jnp.float32).T.astype(jnp.bfloat16)
    halves = [
        jnp.dot(hidden[64 * h : 64 * h + 64], proj_ref[h].reshape(512, E), preferred_element_type=jnp.float32)
        for h in range(2)
    ]
    emb = (halves[0] + halves[1]).astype(jnp.bfloat16)
    for p in range(out_ref.shape[0]):
        out_ref[p] = emb


def small_call(kernel, outs, *args, scratch=(), smem=0, hbm=0, params=PARAMS):
    return pl.pallas_call(
        kernel,
        in_specs=[pl.BlockSpec(memory_space=pltpu.SMEM)] * smem
        + [VM] * (len(args) - smem - hbm)
        + [pl.BlockSpec(memory_space=pl.ANY)] * hbm,
        out_specs=jax.tree.map(lambda _: VM, outs),
        out_shape=outs,
        scratch_shapes=list(scratch),
        compiler_params=params,
    )(*args)


def exchange(x, axes):
    return lax.all_to_all(x, axes, 0, 0, tiled=True)


def swap(x, axis):
    return lax.ppermute(x, axis, [(0, 1), (1, 0)])


def embeddings(buyer_hidden, goods_hidden, buyer_proj, goods_proj, place):
    bf16 = jnp.bfloat16
    shape = jax.ShapeDtypeStruct
    outs = (shape((4, 80, 128), bf16), shape((4, 80, 128), bf16), shape((32, 16, 128), bf16))
    keep, go, tiles = small_call(
        pack_kernel, outs, place, buyer_hidden.T, goods_hidden.T,
        scratch=(pltpu.VMEM((32, 2048), bf16), pltpu.SemaphoreType.DMA), smem=1, hbm=1,
        params=pltpu.CompilerParams(vmem_limit_bytes=61 << 20),
    )
    came = swap(go, "zh")
    here, across = small_call(pair_kernel, (shape((4, 80, 128), bf16),) * 2, keep, came)
    across = swap(across, "c")
    parts = [here[0], across[0]]
    for d in range(1, 4):
        two = jnp.stack([here[d], across[d]])
        two = lax.ppermute(two, "x", [(i, (i + d) % 4) for i in range(4)])
        parts += [two[0], two[1]]
    tiles = exchange(tiles, ("y", "zl"))
    goods_own = small_call(goods_kernel, shape((16, 64, E), bf16), tiles, goods_proj.reshape(32, 2, 16, E).transpose(1, 0, 2, 3))
    goods_emb = exchange(goods_own, RING)
    proj = buyer_proj.reshape(4, 2, 2, 64, E)
    proj = jnp.where(place[1] == 0, proj, proj[:, ::-1]).transpose(0, 2, 1, 3, 4).reshape(8, 128, E)
    buyer_own = small_call(buyers_kernel, shape((32, 80, E), bf16), place, proj, *parts, smem=1)
    buyer_own, goods_emb = lax.optimization_barrier((buyer_own, goods_emb))
    buyer_emb = exchange(buyer_own, PLANE)
    return buyer_emb.reshape(-1, E), goods_emb.reshape(-1, E)


def per_device(buyer_hidden, goods_hidden, buyer_proj, goods_proj, endowment):
    x, y, zh, c = (lax.axis_index(a) for a in ("x", "y", "zh", "c"))
    place = jnp.stack([x, zh, c])
    buyer_emb, goods_emb = embeddings(buyer_hidden, goods_hidden, buyer_proj, goods_proj, place)

    mine = lax.dynamic_index_in_dim(endowment.reshape(4, 2, 160), zh, 1, keepdims=False).reshape(5, 128)
    money_row = lax.dynamic_slice(mine, (jnp.minimum(x * 2 + c, 4), 0), (1, 128))

    values, sent = values_call(goods_emb, buyer_emb, money_row)
    got = exchange(sent, PLANE)
    sent, money = price_call(1, got, values)
    sent, _, square = utility_call(1, exchange(sent, RING), values)
    sent = price_call(2, exchange(sent, PLANE), square, money)
    sent, before, cube = utility_call(2, exchange(sent, RING), values, square)
    got = exchange(sent, PLANE)
    sent = price_call(3, got, cube, money)
    sent, halves = utility_call(3, exchange(sent, RING), before, zh.reshape(1), square)
    final = exchange(sent, PLANE)
    own = lambda a, axis: lax.dynamic_index_in_dim(a, y, axis, keepdims=False)
    before = (own(money, 0) / jnp.sum(own(got, 1), 0)).reshape(5, 128)
    mine_total = jnp.sum(final, 0) * before
    other = swap(mine_total, "zh")
    prices = exchange(lax.optimization_barrier((halves, mine_total))[0], ("y",)).reshape(-1)
    first = jnp.where(zh == 0, mine_total, other).reshape(4, 160)
    second = jnp.where(zh == 0, other, mine_total).reshape(4, 160)
    utility = jnp.stack([first, second], 1).reshape(-1)
    return (prices, utility)


def solution(mesh):
    fine = Mesh(mesh.devices.reshape([n for _, n in FINE]), [a for a, _ in FINE])
    buyers, goods = ("y", "zl"), ("x", "zh", "c")
    placed = (P(buyers, goods), P(goods, buyers), P(), P(), P(buyers))
    return jax.shard_map(
        per_device, mesh=fine, in_specs=placed, out_specs=(P(goods), P(buyers)), check_vma=False
    )
```

```python
import functools

import jax
import jax.numpy as jnp
from jax import lax
from jax.experimental import pallas as pl
from jax.experimental.pallas import tpu as pltpu
from jax.sharding import Mesh, PartitionSpec as P

ITERS = 3
FINE = (("y", 4), ("zl", 8), ("x", 4), ("zh", 2), ("c", 2))
PLANE = ("y", "x", "c")
RING = ("zh", "zl")


E = 128
NBUY = 2560
NGOOD = 1024
LB = NBUY // 128
GT = NGOOD // 128


LOG2E = 1.4426950408889634
LN2 = 0.6931471805599453


def softplus_of(products):
    t = products * (E ** (-0.5) * LOG2E)
    u = jnp.exp2(jnp.minimum(t, 126.0))
    small = u * (LOG2E - (0.5 * LOG2E) * u)
    return jnp.maximum(t, jnp.where(u < 2.0**-8, small, jnp.log2(1.0 + u))) * LN2


def values_kernel(goods_ref, buyers_ref, money_ref, values_ref, out_ref, total, rows):
    step = pl.program_id(0)

    @pl.when(step == 0)
    def _():
        total[...] = jnp.zeros_like(total)

    for b in range(NBUY // 256):
        cols = slice(256 * b, 256 * b + 256)
        scores = lax.dot_general(
            goods_ref[...], buyers_ref[cols, :], (((1,), (1,)), ((), ())), preferred_element_type=jnp.float32
        )
        rounded = softplus_of(scores).astype(jnp.bfloat16)
        values_ref[:, cols] = rounded
        total[:, cols] += jnp.sum(rounded.astype(jnp.float32).reshape(-1, 8, 256), 0)

    @pl.when(step == pl.num_programs(0) - 1)
    def _():
        whole = jnp.sum(total[...], 0, keepdims=True)
        for b in range(LB):
            rows[b : b + 1, :] = whole[:, 128 * b : 128 * b + 128]
        rows[LB : LB + 1, :] = money_ref[...]
        for p in range(out_ref.shape[0]):
            out_ref[p] = rows[0 : LB + 1, :]


def three_parts(x, lhs):
    lhs[...] = jnp.zeros_like(lhs)
    for i in range(3):
        part = x.astype(jnp.bfloat16).astype(jnp.float32)
        x = x - part
        for b in range(part.shape[0]):
            lhs[i : i + 1, 128 * b : 128 * b + 128] = part[b : b + 1, :]


def price_kernel(k, got_ref, *refs):
    if k == 1:
        values, out_ref, money_ref, lhs, money = refs
        for b in range(LB):
            row = got_ref[8 * (b // 5) + b % 5, LB : LB + 1, :]
            money[b : b + 1, :] = row
            money_ref[b // 5 : b // 5 + 1, 128 * (b % 5) : 128 * (b % 5) + 128] = row
        total = got_ref[0, 0:LB, :]
        for p in range(1, got_ref.shape[0]):
            total = total + got_ref[p, 0:LB, :]
        three_parts(money[...] / total, lhs)
        products = lax.dot_general(
            lhs[...].astype(jnp.bfloat16), values[...], (((1,), (1,)), ((), ())), preferred_element_type=jnp.float32
        )
        whole = jnp.sum(products, 0, keepdims=True)
        rows = [whole[:, 128 * q : 128 * q + 128] for q in range(GT)]
    else:
        money_ref, power, out_ref, scale, sums = refs
        total = got_ref[0]
        for p in range(1, got_ref.shape[0]):
            total = total + got_ref[p]
        scale[...] = money_ref[...] / total

        def chunk(i, _):
            at = pl.ds(pl.multiple_of(16 * i, 16), 16)
            two = [None, None]
            for b in range(LB):
                part = scale[b // 5 : b // 5 + 1, 128 * (b % 5) : 128 * (b % 5) + 128]
                term = power[at, 128 * b : 128 * b + 128] * part
                two[b % 2] = term if two[b % 2] is None else two[b % 2] + term
            sums[at, :] = two[0] + two[1]
            return 0

        lax.fori_loop(0, NGOOD // 16, chunk, 0, unroll=4)
        rows = [jnp.sum(sums[128 * q : 128 * q + 128, :].T, 0, keepdims=True) for q in range(GT)]
    for q in range(GT):
        for p in range(out_ref.shape[0]):
            out_ref[p, q : q + 1, :] = rows[q]


def utility_kernel(k, got_ref, *refs):
    if k == 1:
        values, out_ref, sum_ref, power, inverse, rows = refs
    elif k == 2:
        values, square, out_ref, sum_ref, power, inverse, rows = refs
    else:
        before_ref, zh_ref, square, out_ref, prices_ref, inverse, rows = refs
    total = got_ref[0]
    for p in range(1, got_ref.shape[0]):
        total = total + got_ref[p]
    if k == ITERS:
        rows[0:8, :] = total / before_ref[...]
        half = rows[pl.ds(pl.multiple_of(4 * zh_ref[0], 4), 4), :]
        for p in range(prices_ref.shape[0]):
            prices_ref[p] = half
    else:
        sum_ref[...] = total
    ratio = 1.0 / total
    for q in range(GT):
        inverse[128 * q : 128 * q + 128, :] = jnp.broadcast_to(ratio[q : q + 1, :], (128, 128)).T

    def chunk(i, accs):
        at = pl.ds(pl.multiple_of(16 * i, 16), 16)
        c = inverse[at, :]
        new = []
        for b in range(LB):
            cols = slice(128 * b, 128 * b + 128)
            if k == 1:
                v = values[at, cols].astype(jnp.float32)
                raised = v * v
            elif k == 2:
                raised = square[at, cols] * values[at, cols].astype(jnp.float32)
            else:
                v = square[at, cols]
                raised = v * v
            if k < ITERS:
                power[at, cols] = raised
            term = raised * c
            new.append(accs[b] + (term[0:8] + term[8:16]))
        return tuple(new)

    accs = tuple(jnp.zeros((8, 128), jnp.float32) for _ in range(LB))
    accs = lax.fori_loop(0, NGOOD // 16, chunk, accs, unroll=2)
    for b in range(LB):
        row = jnp.sum(accs[b], 0, keepdims=True)
        if k == ITERS:
            rows[b : b + 1, :] = row
        else:
            rows[b // 5 : b // 5 + 1, 128 * (b % 5) : 128 * (b % 5) + 128] = row
    for p in range(out_ref.shape[0]):
        out_ref[p] = rows[5 * (p // 8) : 5 * (p // 8) + 5, :] if k == ITERS else rows[0:4, :]


VM = pl.BlockSpec(memory_space=pltpu.VMEM)
PARAMS = pltpu.CompilerParams(vmem_limit_bytes=16 << 20)


def values_call(goods_emb, buyer_emb, money_row):
    return pl.pallas_call(
        values_kernel,
        grid=(NGOOD // 512,),
        in_specs=[
            pl.BlockSpec((512, E), lambda i: (i, 0)),
            pl.BlockSpec((NBUY, E), lambda i: (0, 0)),
            pl.BlockSpec((1, 128), lambda i: (0, 0)),
        ],
        out_specs=[
            pl.BlockSpec((512, NBUY), lambda i: (i, 0)),
            pl.BlockSpec((32, LB + 1, 128), lambda i: (0, 0, 0)),
        ],
        out_shape=[
            jax.ShapeDtypeStruct((NGOOD, NBUY), jnp.bfloat16),
            jax.ShapeDtypeStruct((32, LB + 1, 128), jnp.float32),
        ],
        scratch_shapes=[pltpu.VMEM((8, NBUY), jnp.float32), pltpu.VMEM((24, 128), jnp.float32)],
        compiler_params=PARAMS,
    )(goods_emb, buyer_emb, money_row)


def price_call(k, got, power, money=None):
    payload = jax.ShapeDtypeStruct((16, GT, 128), jnp.float32)
    first = k == 1
    scratch = [(8, NBUY), (LB, 128)] if first else [(4, 640), (NGOOD, 128)]
    return pl.pallas_call(
        functools.partial(price_kernel, k),
        in_specs=[VM] * (2 if first else 3),
        out_specs=[VM, VM] if first else VM,
        out_shape=[payload, jax.ShapeDtypeStruct((4, 640), jnp.float32)] if first else payload,
        scratch_shapes=[pltpu.VMEM(x, jnp.float32) for x in scratch],
        compiler_params=PARAMS,
    )(*((got, power) if first else (got, money, power)))


def utility_call(k, got, *blocks):
    if k == ITERS:
        outs, specs = [(32, 5, 128), (4, 4, 128)], [VM, VM, pl.BlockSpec(memory_space=pltpu.SMEM), VM]
    else:
        outs, specs = [(32, 4, 640), (GT, 128), (NGOOD, NBUY)], [VM] * (1 + len(blocks))
    return pl.pallas_call(
        functools.partial(utility_kernel, k),
        in_specs=specs,
        out_specs=[VM] * len(outs),
        out_shape=[jax.ShapeDtypeStruct(o, jnp.float32) for o in outs],
        scratch_shapes=[
            pltpu.VMEM((NGOOD, 128), jnp.float32),
            pltpu.VMEM((24, 128) if k == ITERS else (8, 640), jnp.float32),
        ],
        compiler_params=PARAMS,
    )(got, *blocks)


def pack_kernel(place_ref, hidden_ref, goods_ref, keep_ref, go_ref, tiles_ref):
    x, zh, c = place_ref[0], place_ref[1], place_ref[2]
    rows = hidden_ref[...].astype(jnp.float32).T

    def of(to_x, to_zh, to_c):
        at = 80 * (4 * to_x + 2 * to_zh + to_c)
        return rows[at : at + 80]

    for to_x in range(4):
        for to_zh in range(2):
            plain = jnp.concatenate([of(to_x, to_zh, 0), of(to_x, to_zh, 1)], 1)
            turned = jnp.concatenate([of(to_x, to_zh, 1), of(to_x, to_zh, 0)], 1)
            part = jnp.where(c == 0, plain, turned).astype(jnp.bfloat16)
            at = (to_x + 4 - x) & 3

            @pl.when(zh == to_zh)
            def _(at=at, part=part):
                keep_ref[at] = part

            @pl.when(zh != to_zh)
            def _(at=at, part=part):
                go_ref[at] = part

    for t in range(16):
        top = goods_ref[0:16, 128 * t : 128 * t + 128].astype(jnp.float32)
        low = goods_ref[16:32, 128 * t : 128 * t + 128].astype(jnp.float32)
        tiles_ref[2 * t] = jnp.concatenate([top[:, 0:64], low[:, 0:64]], 1).astype(jnp.bfloat16)
        tiles_ref[2 * t + 1] = jnp.concatenate([top[:, 64:128], low[:, 64:128]], 1).astype(jnp.bfloat16)


def pair_kernel(mine_ref, came_ref, here_ref, across_ref):
    for d in range(4):
        mine, came = mine_ref[d].astype(jnp.float32), came_ref[d].astype(jnp.float32)
        here_ref[d] = jnp.concatenate([mine[:, 0:64], came[:, 0:64]], 1).astype(jnp.bfloat16)
        across_ref[d] = jnp.concatenate([mine[:, 64:128], came[:, 64:128]], 1).astype(jnp.bfloat16)


def buyers_kernel(place_ref, proj_ref, *refs):
    got, out_ref = refs[:8], refs[8]
    x, c = place_ref[0], place_ref[2]
    total = jnp.zeros((80, E), jnp.float32)
    for q in range(8):
        at = ((x + 4 - q // 2) & 3) * 2 + ((c + q % 2) & 1)
        total = total + jnp.dot(got[q][...], proj_ref[at], preferred_element_type=jnp.float32)
    emb = total.astype(jnp.bfloat16)
    for p in range(out_ref.shape[0]):
        out_ref[p] = emb


def goods_kernel(got_ref, proj_ref, out_ref):
    hidden = got_ref[...].reshape(512, 128).astype(jnp.float32).T.astype(jnp.bfloat16)
    halves = [
        jnp.dot(hidden[64 * h : 64 * h + 64], proj_ref[h].reshape(512, E), preferred_element_type=jnp.float32)
        for h in range(2)
    ]
    emb = (halves[0] + halves[1]).astype(jnp.bfloat16)
    for p in range(out_ref.shape[0]):
        out_ref[p] = emb


def small_call(kernel, outs, *args, scratch=(), smem=0):
    return pl.pallas_call(
        kernel,
        in_specs=[pl.BlockSpec(memory_space=pltpu.SMEM)] * smem + [VM] * (len(args) - smem),
        out_specs=jax.tree.map(lambda _: VM, outs),
        out_shape=outs,
        scratch_shapes=list(scratch),
        compiler_params=PARAMS,
    )(*args)


def exchange(x, axes):
    return lax.all_to_all(x, axes, 0, 0, tiled=True)


def swap(x, axis):
    return lax.ppermute(x, axis, [(0, 1), (1, 0)])


def embeddings(buyer_hidden, goods_hidden, buyer_proj, goods_proj, place):
    bf16 = jnp.bfloat16
    shape = jax.ShapeDtypeStruct
    outs = (shape((4, 80, 128), bf16), shape((4, 80, 128), bf16), shape((32, 16, 128), bf16))
    keep, go, tiles = small_call(pack_kernel, outs, place, buyer_hidden.T, goods_hidden.T, smem=1)
    came = swap(go, "zh")
    here, across = small_call(pair_kernel, (shape((4, 80, 128), bf16),) * 2, keep, came)
    across = swap(across, "c")
    parts = [here[0], across[0]]
    for d in range(1, 4):
        two = jnp.stack([here[d], across[d]])
        two = lax.ppermute(two, "x", [(i, (i + d) % 4) for i in range(4)])
        parts += [two[0], two[1]]
    tiles = exchange(tiles, ("y", "zl"))
    goods_own = small_call(goods_kernel, shape((16, 64, E), bf16), tiles, goods_proj.reshape(32, 2, 16, E).transpose(1, 0, 2, 3))
    goods_emb = exchange(goods_own, RING)
    proj = buyer_proj.reshape(4, 2, 2, 64, E)
    proj = jnp.where(place[1] == 0, proj, proj[:, ::-1]).transpose(0, 2, 1, 3, 4).reshape(8, 128, E)
    buyer_own = small_call(buyers_kernel, shape((32, 80, E), bf16), place, proj, *parts, smem=1)
    buyer_own, goods_emb = lax.optimization_barrier((buyer_own, goods_emb))
    buyer_emb = exchange(buyer_own, PLANE)
    return buyer_emb.reshape(-1, E), goods_emb.reshape(-1, E)


def per_device(buyer_hidden, goods_hidden, buyer_proj, goods_proj, endowment):
    x, y, zh, c = (lax.axis_index(a) for a in ("x", "y", "zh", "c"))
    place = jnp.stack([x, zh, c])
    buyer_emb, goods_emb = embeddings(buyer_hidden, goods_hidden, buyer_proj, goods_proj, place)

    mine = lax.dynamic_index_in_dim(endowment.reshape(4, 2, 160), zh, 1, keepdims=False).reshape(5, 128)
    money_row = lax.dynamic_slice(mine, (jnp.minimum(x * 2 + c, 4), 0), (1, 128))

    values, sent = values_call(goods_emb, buyer_emb, money_row)
    got = exchange(sent, PLANE)
    sent, money = price_call(1, got, values)
    sent, _, square = utility_call(1, exchange(sent, RING), values)
    sent = price_call(2, exchange(sent, PLANE), square, money)
    sent, before, cube = utility_call(2, exchange(sent, RING), values, square)
    got = exchange(sent, PLANE)
    sent = price_call(3, got, cube, money)
    sent, halves = utility_call(3, exchange(sent, RING), before, zh.reshape(1), square)
    final = exchange(sent, PLANE)
    own = lambda a, axis: lax.dynamic_index_in_dim(a, y, axis, keepdims=False)
    before = (own(money, 0) / jnp.sum(own(got, 1), 0)).reshape(5, 128)
    mine_total = jnp.sum(final, 0) * before
    other = swap(mine_total, "zh")
    prices = exchange(lax.optimization_barrier((halves, mine_total))[0], ("y",)).reshape(-1)
    first = jnp.where(zh == 0, mine_total, other).reshape(4, 160)
    second = jnp.where(zh == 0, other, mine_total).reshape(4, 160)
    utility = jnp.stack([first, second], 1).reshape(-1)
    return (prices, utility)


def solution(mesh):
    fine = Mesh(mesh.devices.reshape([n for _, n in FINE]), [a for a, _ in FINE])
    buyers, goods = ("y", "zl"), ("x", "zh", "c")
    placed = (P(buyers, goods), P(goods, buyers), P(), P(), P(buyers))
    return jax.shard_map(
        per_device, mesh=fine, in_specs=placed, out_specs=(P(goods), P(buyers)), check_vma=False
    )
```
